32 devices in a mesh: ctx: 16 (over z, x, core), kvh: 2 (over y).
Axes of the slice: x: 2, y: 2, z: 4, core: 2. Of those that a mesh axis runs over, the one named last changes fastest.
Arguments:
- doc_lengths: int32 [16], replicated, may hold values from 1 to 384, 4096 in all
- queries: bfloat16 [2, 2048, 2048], P(None, ('ctx', 'kvh')), may hold values from -6 to 6
- key_matrix: bfloat16 [2, 2048, 256], P(None, ('ctx', 'kvh')), may hold values from -6 to 6
- value_matrix: bfloat16 [2, 2048, 256], P(None, ('ctx', 'kvh')), may hold values from -6 to 6
- forward_output: bfloat16 [2, 2048, 2048], P(None, ('ctx', 'kvh')), may hold values from -6 to 6
- output_cotangent: bfloat16 [2, 2048, 2048], P(None, ('ctx', 'kvh')), may hold values from -0.59765625 to 0.59765625
- log_normalizer_rows: float32 [2, 2048, 16], P(None, ('ctx', 'kvh')), may hold values from 1.5 to 3
Outputs:
- query_gradient: bfloat16 [2, 2048, 2048], P(None, 'ctx', 'kvh')
- key_gradient: bfloat16 [2, 2048, 256], P(None, 'ctx', 'kvh')
- value_gradient: bfloat16 [2, 2048, 256], P(None, 'ctx', 'kvh')
The draws below stay inside these ranges and needn't reach their ends.
Inputs may be any that keep to these rules, and one draw needn't show every extreme that they name: `doc_lengths`: the documents fill the pack of 4096 positions end to end; the longest has exactly 384 tokens.
All inputs are finite; a program needn't handle non-finite values.
Results may differ from the reference program's by a relative error of at most 0.0054.
Values may be sent and summed in bfloat16 or wider, within the bound.
A program may use at most 64 MiB of HBM per device.

```python
import math
from functools import partial
import jax
import jax.numpy as jnp
import numpy as np
from jax import lax

QUERY_PER_GROUP = 8
HEAD_SIZE = 128
BLOCK_TOKENS = 128
LOOK = 3
KEY_VALUE_HEADS = 2
HQ = 16
HALF_TOKENS = 2048
DOCMAX = 384
DOCS = 16
N_CTX = 16


def block_scale(own_key, shape, split, least, high):
    def one(dim, parts):
        draws = jax.random.uniform(jax.random.fold_in(jax.random.fold_in(own_key, 6), dim), (parts,), jnp.float32, least / len(split), high / len(split))
        return jnp.repeat(jnp.exp(draws), shape[dim] // parts).reshape((-1,) + (1,) * (len(shape) - dim - 1))

    factor_of = one(*split[0])
    for cut in split[1:]:
        factor_of = factor_of * one(*cut)
    return factor_of


def profile(count, total, reach, skew):
    weights = [(1 << 20) // math.isqrt(grade ** skew) + 1 for grade in range(2, count + 1)]
    rest, holding = total - reach - (count - 1), [1] * (count - 1)
    while rest > 0:
        movable = [i for i in range(count - 1) if holding[i] < reach]
        mass, left = sum([weights[i] for i in movable]), rest
        for i in movable:
            extra = min(reach - holding[i], max(1, left * weights[i] // mass), rest)
            holding[i] = holding[i] + extra
            rest = rest - extra
    return np.array([reach] + holding)


def uneven_parts(own_key, amount, total, most, skew):
    if amount == 2:
        one = jax.random.randint(own_key, (), max(1, total - most), min(most, total - 1) + 1)
        return jnp.stack([one, total - one])
    tallies = jnp.asarray(profile(amount, total, most, skew), jnp.int32)
    twos = (amount - 1) // 2
    giver, sink = tallies[1:1 + 2 * twos:2], tallies[2:2 + 2 * twos:2]
    room = jnp.minimum(giver - 1, most - sink)
    moved = jax.random.randint(jax.random.fold_in(own_key, 1), (twos,), 0, 1 << 20) % (room + 1)
    tallies = tallies.at[1:1 + 2 * twos:2].set(giver - moved).at[2:2 + 2 * twos:2].set(sink + moved)
    return tallies[jax.random.permutation(jax.random.fold_in(own_key, 2), amount)]


def scatter_about(stream_key, extent, width, reach, pieces=(), held_as=jnp.bfloat16):
    values = jax.random.normal(stream_key, extent, jnp.float32) * width
    if len(pieces) > 0:
        values = block_scale(stream_key, extent, pieces, -0.22, 0.18) * values
    return jnp.clip(values, min=-reach, max=reach).astype(held_as)


def setup_inputs(seed: int = 0) -> dict:
    key_of = jax.random.split(jax.random.key(seed), 8)
    doc_lengths = uneven_parts(key_of[0], DOCS, 2 * N_CTX * BLOCK_TOKENS, DOCMAX, 1).astype(jnp.int32)
    queries = scatter_about(key_of[1], (2, HALF_TOKENS, HQ * HEAD_SIZE), 1.0, 6.0, ((1, 32),))
    key_matrix = scatter_about(key_of[2], (2, HALF_TOKENS, KEY_VALUE_HEADS * HEAD_SIZE), 1.0, 6.0, ((1, 32),))
    value_matrix = scatter_about(key_of[3], (2, HALF_TOKENS, KEY_VALUE_HEADS * HEAD_SIZE), 1.0, 6.0, ((1, 32),))
    forward_output = scatter_about(key_of[4], (2, HALF_TOKENS, HQ * HEAD_SIZE), 1.0, 6.0, ((1, 32),))
    output_cotangent = scatter_about(key_of[5], (2, HALF_TOKENS, HQ * HEAD_SIZE), 0.1, 0.59765625, ((1, 32),))
    log_normalizer_rows = jnp.clip(1.5 + 1.5 * jax.random.uniform(key_of[6], (2, HALF_TOKENS, HQ), jnp.float32) ** block_scale(key_of[6], (2, HALF_TOKENS, HQ), ((1, 32),), -0.2, 0.2), 1.5, 3.0)
    return dict(doc_lengths=doc_lengths, queries=queries, key_matrix=key_matrix, value_matrix=value_matrix, forward_output=forward_output, output_cotangent=output_cotangent, log_normalizer_rows=log_normalizer_rows)


def spread_rows(array):
    upper_half = array[1].reshape((N_CTX, BLOCK_TOKENS) + array.shape[2:])[::-1].reshape(array.shape[1:])
    return jnp.concatenate([array[0], upper_half], axis=0)


def fold_back_rows(array):
    half_len = array.shape[0] // 2
    upper_half = array[half_len:].reshape((N_CTX, BLOCK_TOKENS) + array.shape[1:])[::-1].reshape((half_len,) + array.shape[1:])
    return jnp.stack([array[:half_len], upper_half])


def tile_grads(query_tile, grad_tile, norm_tile, delta_tile, key_tile, value_tile, allowed):
    inv_root = HEAD_SIZE ** -0.5
    scores = jnp.einsum("qhgd,khd->hgqk", query_tile, key_tile) * inv_root
    weights = jnp.where(allowed[None, None], jnp.exp(scores - norm_tile[:, :, :, None]), 0.0)
    weight_bf = lax.optimization_barrier(weights.astype(jnp.bfloat16)).astype(jnp.float32)
    value_gradient = jnp.einsum("hgqk,qhgd->khd", weight_bf, grad_tile)
    weight_grad = jnp.einsum("qhgd,khd->hgqk", grad_tile, value_tile)
    score_grad = weights * (weight_grad - delta_tile[:, :, :, None])
    score_bf = lax.optimization_barrier(score_grad.astype(jnp.bfloat16)).astype(jnp.float32)
    query_gradient = jnp.einsum("hgqk,khd->qhgd", score_bf, key_tile) * inv_root
    key_gradient = jnp.einsum("hgqk,qhgd->khd", score_bf, query_tile) * inv_root
    return query_gradient, key_gradient, value_gradient


def empty_grads():
    return (jnp.zeros((BLOCK_TOKENS, KEY_VALUE_HEADS, QUERY_PER_GROUP, HEAD_SIZE), jnp.float32), jnp.zeros((BLOCK_TOKENS, KEY_VALUE_HEADS, HEAD_SIZE), jnp.float32), jnp.zeros((BLOCK_TOKENS, KEY_VALUE_HEADS, HEAD_SIZE), jnp.float32))


def reference(doc_lengths, queries, key_matrix, value_matrix, forward_output, output_cotangent, log_normalizer_rows):
    sequence_length = 2 * N_CTX * BLOCK_TOKENS
    padding_length = LOOK * BLOCK_TOKENS
    query_full = spread_rows(queries).astype(jnp.float32).reshape(sequence_length, KEY_VALUE_HEADS, QUERY_PER_GROUP, HEAD_SIZE)
    gradient_full = spread_rows(output_cotangent).astype(jnp.float32).reshape(sequence_length, KEY_VALUE_HEADS, QUERY_PER_GROUP, HEAD_SIZE)
    output_full = spread_rows(forward_output).astype(jnp.float32).reshape(sequence_length, KEY_VALUE_HEADS, QUERY_PER_GROUP, HEAD_SIZE)
    delta_all = jnp.sum(gradient_full * output_full, axis=-1)
    norm_full = spread_rows(log_normalizer_rows).reshape(sequence_length, KEY_VALUE_HEADS, QUERY_PER_GROUP)
    key_full = jnp.pad(spread_rows(key_matrix).astype(jnp.float32).reshape(sequence_length, KEY_VALUE_HEADS, HEAD_SIZE), ((padding_length, 0), (0, 0), (0, 0)))
    value_full = jnp.pad(spread_rows(value_matrix).astype(jnp.float32).reshape(sequence_length, KEY_VALUE_HEADS, HEAD_SIZE), ((padding_length, 0), (0, 0), (0, 0)))
    doc_ends = jnp.cumsum(doc_lengths)
    position = jnp.arange(sequence_length, dtype=jnp.int32)
    doc_ids = jnp.sum((doc_ends[None, :] <= position[:, None]).astype(jnp.int32), axis=1)
    key_docs = jnp.concatenate([jnp.full((padding_length,), -1, jnp.int32), doc_ids])
    key_pos = jnp.arange(sequence_length + padding_length, dtype=jnp.int32) - padding_length

    def block_step(grad_sums, block_id):
        key_gradient_totals, value_gradient_totals = grad_sums
        row_start = block_id * BLOCK_TOKENS
        query_tile = lax.dynamic_slice_in_dim(query_full, row_start, BLOCK_TOKENS, 0)
        grad_tile = lax.dynamic_slice_in_dim(gradient_full, row_start, BLOCK_TOKENS, 0)
        norm_tile = jnp.transpose(lax.dynamic_slice_in_dim(norm_full, row_start, BLOCK_TOKENS, 0), (1, 2, 0))
        delta_tile = jnp.transpose(lax.dynamic_slice_in_dim(delta_all, row_start, BLOCK_TOKENS, 0), (1, 2, 0))
        query_docs = lax.dynamic_slice_in_dim(doc_ids, row_start, BLOCK_TOKENS, 0)
        query_pos = row_start + jnp.arange(BLOCK_TOKENS, dtype=jnp.int32)
        query_total = jnp.zeros((BLOCK_TOKENS, KEY_VALUE_HEADS, QUERY_PER_GROUP, HEAD_SIZE), jnp.float32)
        for lookback in range(LOOK + 1):
            key_start = row_start + (LOOK - lookback) * BLOCK_TOKENS
            key_tile = lax.dynamic_slice_in_dim(key_full, key_start, BLOCK_TOKENS, 0)
            value_tile = lax.dynamic_slice_in_dim(value_full, key_start, BLOCK_TOKENS, 0)
            tile_docs = lax.dynamic_slice_in_dim(key_docs, key_start, BLOCK_TOKENS, 0)
            tile_pos = lax.dynamic_slice_in_dim(key_pos, key_start, BLOCK_TOKENS, 0)
            same_doc = query_docs[:, None] == tile_docs[None, :]
            allowed = same_doc & (tile_pos[None, :] <= query_pos[:, None])
            compute = partial(tile_grads, query_tile, grad_tile, norm_tile, delta_tile, key_tile, value_tile, allowed)
            query_part, key_part, value_part = lax.cond(jnp.any(same_doc), compute, empty_grads)
            query_total = query_total + query_part
            key_gradient_totals = lax.dynamic_update_slice_in_dim(key_gradient_totals, lax.dynamic_slice_in_dim(key_gradient_totals, key_start, BLOCK_TOKENS, 0) + key_part, key_start, 0)
            value_gradient_totals = lax.dynamic_update_slice_in_dim(value_gradient_totals, lax.dynamic_slice_in_dim(value_gradient_totals, key_start, BLOCK_TOKENS, 0) + value_part, key_start, 0)
        return (key_gradient_totals, value_gradient_totals), query_total

    initial_totals = (jnp.zeros((sequence_length + padding_length, KEY_VALUE_HEADS, HEAD_SIZE), jnp.float32), jnp.zeros((sequence_length + padding_length, KEY_VALUE_HEADS, HEAD_SIZE), jnp.float32))
    (key_gradient_totals, value_gradient_totals), query_gradient_totals = lax.scan(block_step, initial_totals, jnp.arange(2 * N_CTX, dtype=jnp.int32))
    query_gradient = fold_back_rows(query_gradient_totals.reshape(sequence_length, KEY_VALUE_HEADS * QUERY_PER_GROUP * HEAD_SIZE).astype(jnp.bfloat16))
    key_gradient = fold_back_rows(key_gradient_totals[padding_length:].reshape(sequence_length, KEY_VALUE_HEADS * HEAD_SIZE).astype(jnp.bfloat16))
    value_gradient = fold_back_rows(value_gradient_totals[padding_length:].reshape(sequence_length, KEY_VALUE_HEADS * HEAD_SIZE).astype(jnp.bfloat16))
    return query_gradient, key_gradient, value_gradient
```

```python
import functools

import jax
import jax.numpy as jnp
from jax import lax
from jax.experimental import pallas as pl
from jax.experimental.pallas import tpu as pltpu
from jax.sharding import PartitionSpec as P

LOOK = 3
MESH = pl.DeviceIdType.MESH
F32 = jnp.float32
BF16 = jnp.bfloat16
NT = (((1,), (1,)), ((), ()))


def row_sums(values, terms):
    ones = jnp.ones((8, values.shape[1]), BF16)
    total, rest = None, values
    for _ in range(terms):
        part = rest.astype(BF16)
        rest = rest - part.astype(F32)
        term = lax.dot_general(ones, part, NT, preferred_element_type=F32)
        total = term if total is None else total + term
    return total


def kernel(
    dims,
    docs_ref, lse_ref, q_hbm, k_hbm, v_hbm, o_hbm, g_hbm,
    dqo, dk_ref, dv_ref,
    qb, gb, gl, ol, kvb, ktb, dk_acc, dv_acc, sb, rb, aux_s, aux_r,
    loc_sem, kvl_sem, y_send, y_recv, kvy_send, kvy_recv, kv_send, kv_recv,
    aux_send_sem, aux_recv_sem, d_send, d_recv,
):
    n_ctx, n_kvh, rows, group, size, chunk_heads, n_docs = dims
    block = n_kvh * rows
    width = group * size
    chunks = group // chunk_heads
    lanes = chunk_heads * rows
    n_blocks = 2 * n_ctx
    scale = size ** -0.5
    c = lax.axis_index("ctx")
    h = lax.axis_index("kvh")
    ids = (c, n_blocks - 1 - c)
    odd = lax.rem(c, 2)
    pair = c + 1 - 2 * odd
    even = (odd == 0, odd == 1)
    others = [lax.rem(h + i, n_kvh) for i in range(1, n_kvh)]

    def place(b):
        return jnp.where(b < n_ctx, b, n_blocks - 1 - b), jnp.where(b < n_ctx, 0, 1)

    def mult(x, m):
        return pl.multiple_of(x, m)

    def tile(j, p=None):
        if p is None:
            return pl.ds(mult(j * block, block), block)
        return pl.ds(mult(j * block + p * rows, rows), rows)

    own_cols = pl.ds(mult(h * width, width), width)
    own_key = pl.ds(mult(h * size, size), size)
    kv_local = []
    for s in range(2):
        for a, src in enumerate((k_hbm, v_hbm)):
            cp = pltpu.make_async_copy(
                src.at[s, :, own_key],
                kvb.at[s, tile(LOOK, h), pl.ds(a * size, size)],
                kvl_sem.at[s, a],
            )
            cp.start()
            kv_local.append(cp)
    local = [
        pltpu.make_async_copy(g_hbm, gl, loc_sem.at[0]),
        pltpu.make_async_copy(o_hbm, ol, loc_sem.at[1]),
        pltpu.make_async_copy(q_hbm.at[:, :, own_cols], qb.at[:, h], loc_sem.at[2]),
        pltpu.make_async_copy(g_hbm.at[:, :, own_cols], gb.at[:, h], loc_sem.at[3]),
    ]
    for cp in local:
        cp.start()

    barrier = pltpu.get_barrier_semaphore()
    count = jnp.int32(n_kvh)
    for t in others:
        pl.semaphore_signal(barrier, inc=1, device_id={"kvh": t}, device_id_type=MESH)
    pl.semaphore_signal(barrier, inc=1, device_id={"ctx": pair}, device_id_type=MESH)
    for ctx in (c - 2, c + 2, c - 3 + 6 * odd):
        inside = (ctx >= 0) & (ctx < n_ctx)
        count = count + inside.astype(jnp.int32)

        @pl.when(inside)
        def _():
            pl.semaphore_signal(barrier, inc=1, device_id={"ctx": ctx}, device_id_type=MESH)

    for s in range(2):
        for d in range(1, LOOK + 1):
            @pl.when(ids[s] - d < 0)
            def _():
                kvb[s, (LOOK - d) * block:(LOOK - d + 1) * block, :] = jnp.zeros(
                    (block, 2 * size), BF16
                )
    pl.semaphore_wait(barrier, count)

    kvy, ysent, auxsent, sent = [], [], [], []
    for s in range(2):
        for i, t in enumerate(others):
            for a, src in enumerate((k_hbm, v_hbm)):
                cp = pltpu.make_async_remote_copy(
                    src.at[s, :, pl.ds(mult(t * size, size), size)],
                    kvb.at[s, tile(LOOK, h), pl.ds(a * size, size)],
                    kvy_send.at[s, i, a],
                    kvy_recv.at[s, h],
                    device_id={"kvh": t},
                    device_id_type=MESH,
                )
                cp.start()
                kvy.append(cp)

    def send_chunk(s, k):
        for i, t in enumerate(others):
            for a, (src, dst) in enumerate(((q_hbm, qb), (g_hbm, gb))):
                span = chunk_heads * size
                cp = pltpu.make_async_remote_copy(
                    src.at[s, :, pl.ds(mult(t * width + k * span, span), span)],
                    dst.at[s, h, :, pl.ds(k * span, span)],
                    y_send.at[s, k, i, a],
                    y_recv.at[s, k, h, a],
                    device_id={"kvh": t},
                    device_id_type=MESH,
                )
                cp.start()
                ysent.append(cp)

    def send(valid, src, dst, send_sem, recv_sem, ctx):
        cp = pltpu.make_async_remote_copy(
            src, dst, send_sem, recv_sem, device_id={"ctx": ctx}, device_id_type=MESH
        )
        pl.when(valid)(cp.start)
        sent.append((valid, cp))

    def spread_part(s, p, i):
        b, src = ids[s], kvb.at[s, tile(LOOK, p), :]
        ctx, half = place(b + 2)
        send(
            b + 2 < n_blocks, src, kvb.at[half, tile(1, p), :],
            kv_send.at[s, 0, i], kv_recv.at[half, 1, p], ctx,
        )
        ctx, half = place(b + 3)
        j = jnp.where(even[s], 2, 0)
        ctx, half = jnp.where(even[s], pair, ctx), jnp.where(even[s], s, half)
        send(
            even[s] | (b + 3 < n_blocks), src, kvb.at[half, tile(j, p), :],
            kv_send.at[s, 1, i], kv_recv.at[half, j, p], ctx,
        )

    def wait_part(s, j, p):
        part = kvb.at[s, tile(j, p), :]
        pl.when(ids[s] - (LOOK - j) >= 0)(
            pltpu.make_async_copy(part, part, kv_recv.at[s, j, p]).wait
        )

    def forward_part(s, p, i):
        wait_part(s, 1, p)
        j = jnp.where(even[s], 0, 2)
        send(
            ids[s] >= 2, kvb.at[s, tile(1, p), :], kvb.at[s, tile(j, p), :],
            kv_send.at[s, 2, i], kv_recv.at[s, j, p], pair,
        )

    send_chunk(0, 0)
    for cp in kv_local:
        cp.wait()
    for s in range(2):
        spread_part(s, h, 0)

    local[0].wait()
    local[1].wait()

    def fill_aux(g):
        cols = pl.ds(mult(g * width, width), width)
        for s in range(2):
            prods = gl[s, :, cols].astype(F32) * ol[s, :, cols].astype(F32)
            delta = row_sums(
                jnp.concatenate([prods[:, i * size:(i + 1) * size] for i in range(group)], axis=0), 2
            )
            for k in range(chunks):
                r = 2 * (s * chunks + k)
                aux_s[g, r + 1:r + 2, :] = delta[:1, k * lanes:(k + 1) * lanes]
                lse = lse_ref[s, pl.ds(mult(g * group + k * chunk_heads, chunk_heads), chunk_heads), :]
                for i in range(chunk_heads):
                    aux_s[g, r:r + 1, i * rows:(i + 1) * rows] = lse[i:i + 1]

    for i, t in enumerate(others):
        fill_aux(t)
        cp = pltpu.make_async_remote_copy(
            aux_s.at[t], aux_r.at[h], aux_send_sem.at[i], aux_recv_sem.at[h],
            device_id={"kvh": t}, device_id_type=MESH,
        )
        cp.start()
        auxsent.append(cp)
    for s in range(2):
        for k in range(chunks):
            if s + k:
                send_chunk(s, k)
    for s in range(2):
        for i, t in enumerate(others):
            part = kvb.at[s, tile(LOOK, t), :]
            pltpu.make_async_copy(part, part, kvy_recv.at[s, t]).wait()
            spread_part(s, t, i + 1)
    fill_aux(h)
    aux_r[h] = aux_s[h]

    own_span = slice(LOOK * block, (LOOK + 1) * block)
    ends, total = [], jnp.int32(0)
    for i in range(n_docs):
        total = total + docs_ref[i]
        ends.append(total)
    spot = lax.broadcasted_iota(jnp.int32, (1, lanes), 1) % rows
    key_spot = lax.broadcasted_iota(jnp.int32, (block, lanes), 0)

    def stage(s, slot, dk, dv):
        sb[s, slot, :, :size] = (dk * scale).astype(BF16)
        sb[s, slot, :, size:] = dv.astype(BF16)

    def send_exchange(s, j):
        stage(s, 0, dk_acc[s, tile(j), :], dv_acc[s, tile(j), :])
        send(ids[s] >= 2, sb.at[s, 0], rb.at[s, 2], d_send.at[s, 0], d_recv.at[s, 2], pair)

    def send_direct(s, j):
        stage(s, 1, dk_acc[s, tile(j), :], dv_acc[s, tile(j), :])
        b = ids[s]
        ctx, half = place(b - 3)
        ctx, half = jnp.where(even[s], ctx, pair), jnp.where(even[s], half, s)
        send(
            (~even[s]) | (b - 3 >= 0), sb.at[s, 1], rb.at[half, 1],
            d_send.at[s, 1], d_recv.at[half, 1], ctx,
        )

    def send_combined(s):
        b = ids[s]
        ctx, half = place(b - 2)

        @pl.when(b >= 2)
        def _():
            pltpu.make_async_copy(rb.at[s, 2], rb.at[s, 2], d_recv.at[s, 2]).wait()
            sb[s, 2, :, :size] = (
                dk_acc[s, block:2 * block, :] * scale + rb[s, 2, :, :size].astype(F32)
            ).astype(BF16)
            sb[s, 2, :, size:] = (
                dv_acc[s, block:2 * block, :] + rb[s, 2, :, size:].astype(F32)
            ).astype(BF16)

        send(b >= 2, sb.at[s, 2], rb.at[half, 0], d_send.at[s, 2], d_recv.at[half, 0], ctx)

    def compute(s, p, k, first, last, tiles, dqt=None, finish=True):
        heads = range(k * chunk_heads, (k + 1) * chunk_heads)
        q = jnp.concatenate([qb[s, p, :, n * size:(n + 1) * size] for n in heads], axis=0)
        g = jnp.concatenate([gb[s, p, :, n * size:(n + 1) * size] for n in heads], axis=0)
        r = 2 * (s * chunks + k)
        norm = aux_r[p, r:r + 1, :]
        delta = aux_r[p, r + 1:r + 2, :]
        pos = ids[s] * block + p * rows + spot
        start = jnp.zeros_like(pos)
        for end in ends:
            start = jnp.where(pos >= end, end, start)
        base = (ids[s] - LOOK) * block
        pos, start = pos - base, start - base
        if last:
            tiles = [jnp.where(even[s], 2, 0), jnp.where(even[s], 0, 2), 1, LOOK]
        for i, j in enumerate(tiles):
            span = tile(j)
            st = lax.dot_general(kvb[s, span, :size], q, NT, preferred_element_type=F32)
            t = key_spot + j * block
            allowed = t >= start
            if isinstance(j, int) and j == LOOK:
                allowed = allowed & (t <= pos)
            w = jnp.where(allowed, jnp.exp(st * scale - norm), 0.0)
            dv = jnp.dot(w.astype(BF16), g, preferred_element_type=F32)
            dp = lax.dot_general(kvb[s, span, size:], g, NT, preferred_element_type=F32)
            ds = (w * (dp - delta)).astype(BF16)
            dk = jnp.dot(ds, q, preferred_element_type=F32)
            if first:
                dv_acc[s, span, :] = dv
                dk_acc[s, span, :] = dk
            else:
                dv_acc[s, span, :] += dv
                dk_acc[s, span, :] += dk
            if last and i == 0:
                send_exchange(s, j)
            if last and i == 1:
                send_direct(s, j)
            part = jnp.dot(ktb[s, :, span], ds, preferred_element_type=F32)
            dqt = part if dqt is None else dqt + part
        if last:
            send_combined(s)
        if not finish:
            return dqt
        dq = (jnp.transpose(dqt) * scale).astype(BF16)
        for i, n in enumerate(heads):
            dqo[s, pl.ds(mult(p * rows, rows), rows), n * size:(n + 1) * size] = dq[i * rows:(i + 1) * rows]

    local[2].wait()
    local[3].wait()
    started = {}
    for s in range(2):
        forward_part(s, h, 0)
    for s in range(2):
        ktb[s, :, own_span] = jnp.transpose(kvb[s, own_span, :size])
        for k in range(chunks):
            started[s, k] = compute(s, h, k, k == 0, False, [LOOK], None, False)
        for i, t in enumerate(others):
            forward_part(s, t, i + 1)
    for s in range(2):
        for j in (0, 2):
            for p in range(n_kvh):
                wait_part(s, j, p)
        ktb[s, :, :LOOK * block] = jnp.transpose(kvb[s, :LOOK * block, :size])
        for k in range(chunks):
            compute(s, h, k, k == 0, False, range(LOOK), started[s, k])

    for i, t in enumerate(others):
        pltpu.make_async_copy(aux_r.at[t], aux_r.at[t], aux_recv_sem.at[t]).wait()
    for s in range(2):
        for k in range(chunks):
            for i, t in enumerate(others):
                for a, buf in enumerate((qb, gb)):
                    part = buf.at[s, t, :, pl.ds(k * chunk_heads * size, chunk_heads * size)]
                    pltpu.make_async_copy(part, part, y_recv.at[s, k, t, a]).wait()
                compute(s, t, k, False, k == chunks - 1 and i == n_kvh - 2, range(LOOK + 1))

    for s in range(2):
        own = slice(LOOK * block, (LOOK + 1) * block)
        b = ids[s]
        dk_acc[s, own, :] = dk_acc[s, own, :] * scale
        for slot, valid in ((1, even[s] | (b + 3 < n_blocks)), (0, b + 2 < n_blocks)):
            @pl.when(valid)
            def _():
                pltpu.make_async_copy(rb.at[s, slot], rb.at[s, slot], d_recv.at[s, slot]).wait()
                dk_acc[s, own, :] += rb[s, slot, :, :size].astype(F32)
                dv_acc[s, own, :] += rb[s, slot, :, size:].astype(F32)

        dk_ref[s] = dk_acc[s, own, :].astype(BF16)
        dv_ref[s] = dv_acc[s, own, :].astype(BF16)

    for cp in kvy + ysent + auxsent:
        cp.wait_send()
    for valid, cp in sent:
        pl.when(valid)(cp.wait_send)


def write_out(*refs):
    copies = [
        pltpu.make_async_copy(refs[i], refs[3 + i], refs[6].at[i]) for i in range(3)
    ]
    for cp in copies:
        cp.start()
    for cp in copies:
        cp.wait()


def body(
    doc_lengths,
    queries,
    key_matrix,
    value_matrix,
    forward_output,
    output_cotangent,
    log_normalizer_rows,
):
    n_ctx, n_kvh = lax.axis_size("ctx"), lax.axis_size("kvh")
    rows = queries.shape[1]
    group = queries.shape[2] // key_matrix.shape[2]
    size = key_matrix.shape[2] // n_kvh
    block = rows * n_kvh
    width = group * size
    chunk_heads = max(1, min(group, 256 // rows))
    chunks = group // chunk_heads
    dims = (n_ctx, n_kvh, rows, group, size, chunk_heads, doc_lengths.shape[0])
    peers = n_kvh - 1
    lanes = chunk_heads * rows
    aux_rows = -(-4 * chunks // 8) * 8
    dma = pltpu.SemaphoreType.DMA
    anywhere = pl.BlockSpec(memory_space=pl.ANY)
    vmem = pl.BlockSpec(memory_space=pltpu.VMEM)
    grads = pl.pallas_call(
        functools.partial(kernel, dims),
        out_shape=(
            pltpu.VMEM((2, block, width), BF16),
            pltpu.VMEM((2, block, size), BF16),
            pltpu.VMEM((2, block, size), BF16),
        ),
        in_specs=[pl.BlockSpec(memory_space=pltpu.SMEM), vmem] + [anywhere] * 5,
        out_specs=(vmem, vmem, vmem),
        scratch_shapes=[
            pltpu.VMEM((2, n_kvh, rows, width), BF16),
            pltpu.VMEM((2, n_kvh, rows, width), BF16),
            pltpu.VMEM((2, rows, width * n_kvh), BF16),
            pltpu.VMEM((2, rows, width * n_kvh), BF16),
            pltpu.VMEM((2, (LOOK + 1) * block, 2 * size), BF16),
            pltpu.VMEM((2, size, (LOOK + 1) * block), BF16),
            pltpu.VMEM((2, (LOOK + 1) * block, size), F32),
            pltpu.VMEM((2, (LOOK + 1) * block, size), F32),
            pltpu.VMEM((2, 3, block, 2 * size), BF16),
            pltpu.VMEM((2, 3, block, 2 * size), BF16),
            pltpu.VMEM((n_kvh, aux_rows, lanes), F32),
            pltpu.VMEM((n_kvh, aux_rows, lanes), F32),
            dma((4,)),
            dma((2, 2)),
            dma((2, chunks, peers, 2)),
            dma((2, chunks, n_kvh, 2)),
            dma((2, peers, 2)),
            dma((2, n_kvh)),
            dma((2, 3, n_kvh)),
            dma((2, LOOK, n_kvh)),
            dma((peers,)),
            dma((n_kvh,)),
            dma((2, 3)),
            dma((2, 3)),
        ],
        compiler_params=pltpu.CompilerParams(collective_id=0, has_side_effects=True),
    )(
        doc_lengths, jnp.transpose(log_normalizer_rows, (0, 2, 1)), queries, key_matrix, value_matrix,
        forward_output, output_cotangent,
    )
    return pl.pallas_call(
        write_out,
        out_shape=tuple(jax.ShapeDtypeStruct(x.shape, x.dtype) for x in grads),
        in_specs=[vmem] * 3,
        out_specs=[anywhere] * 3,
        scratch_shapes=[dma((3,))],
    )(*[pltpu.with_memory_space_constraint(x, pltpu.VMEM) for x in grads])


def solution(mesh):
    rows = P(None, ("ctx", "kvh"), None)
    return jax.shard_map(
        body,
        mesh=mesh,
        in_specs=(P(),) + (rows,) * 6,
        out_specs=(P(None, "ctx", "kvh"),) * 3,
        check_vma=False,
    )
```

```python
import functools

import jax
import jax.numpy as jnp
from jax import lax
from jax.experimental import pallas as pl
from jax.experimental.pallas import tpu as pltpu
from jax.sharding import PartitionSpec as P

LOOK = 3
MESH = pl.DeviceIdType.MESH
F32 = jnp.float32
BF16 = jnp.bfloat16
NT = (((1,), (1,)), ((), ()))


def row_sums(values, terms):
    ones = jnp.ones((8, values.shape[1]), BF16)
    total, rest = None, values
    for _ in range(terms):
        part = rest.astype(BF16)
        rest = rest - part.astype(F32)
        term = lax.dot_general(ones, part, NT, preferred_element_type=F32)
        total = term if total is None else total + term
    return total


def kernel(
    dims,
    docs_ref, lse_ref, q_hbm, k_hbm, v_hbm, o_hbm, g_hbm,
    dqo, dk_ref, dv_ref,
    qb, gb, gl, ol, kvb, ktb, dk_acc, dv_acc, sb, rb, aux_s, aux_r,
    loc_sem, kvl_sem, y_send, y_recv, kvy_send, kvy_recv, kv_send, kv_recv,
    aux_send_sem, aux_recv_sem, d_send, d_recv, gate,
):
    n_ctx, n_kvh, rows, group, size, chunk_heads, n_docs = dims
    block = n_kvh * rows
    width = group * size
    chunks = group // chunk_heads
    lanes = chunk_heads * rows
    n_blocks = 2 * n_ctx
    scale = size ** -0.5
    c = lax.axis_index("ctx")
    h = lax.axis_index("kvh")
    ids = (c, n_blocks - 1 - c)
    odd = lax.rem(c, 2)
    pair = c + 1 - 2 * odd
    even = (odd == 0, odd == 1)
    others = [lax.rem(h + i, n_kvh) for i in range(1, n_kvh)]

    def place(b):
        return jnp.where(b < n_ctx, b, n_blocks - 1 - b), jnp.where(b < n_ctx, 0, 1)

    def mult(x, m):
        return pl.multiple_of(x, m)

    def tile(j, p=None):
        if p is None:
            return pl.ds(mult(j * block, block), block)
        return pl.ds(mult(j * block + p * rows, rows), rows)

    barrier = pltpu.get_barrier_semaphore()
    leader = n_kvh - 1

    def signal(sem, **device):
        pl.semaphore_signal(sem, inc=1, device_id=device, device_id_type=MESH)

    @pl.when(h != leader)
    def _():
        signal(barrier, kvh=leader)

    @pl.when(h == leader)
    def _():
        if leader:
            pl.semaphore_wait(barrier, leader)
        for t in range(leader):
            signal(gate.at[0], kvh=t)

    @pl.when(h != leader)
    def _():
        pl.semaphore_wait(gate.at[0], 1)

    kvy, ysent, auxsent, sent = [], [], [], []
    for s in range(2):
        for i, t in enumerate(others):
            for a, src in enumerate((k_hbm, v_hbm)):
                cp = pltpu.make_async_remote_copy(
                    src.at[s, :, pl.ds(mult(t * size, size), size)],
                    kvb.at[s, tile(LOOK, h), pl.ds(a * size, size)],
                    kvy_send.at[s, i, a],
                    kvy_recv.at[s, h],
                    device_id={"kvh": t},
                    device_id_type=MESH,
                )
                cp.start()
                kvy.append(cp)

    def send_chunk(s, k):
        for i, t in enumerate(others):
            for a, (src, dst) in enumerate(((q_hbm, qb), (g_hbm, gb))):
                span = chunk_heads * size
                cp = pltpu.make_async_remote_copy(
                    src.at[s, :, pl.ds(mult(t * width + k * span, span), span)],
                    dst.at[s, h, :, pl.ds(k * span, span)],
                    y_send.at[s, k, i, a],
                    y_recv.at[s, k, h, a],
                    device_id={"kvh": t},
                    device_id_type=MESH,
                )
                cp.start()
                ysent.append(cp)

    send_chunk(0, 0)
    own_cols = pl.ds(mult(h * width, width), width)
    own_key = pl.ds(mult(h * size, size), size)
    kv_local = []
    for s in range(2):
        for a, src in enumerate((k_hbm, v_hbm)):
            cp = pltpu.make_async_copy(
                src.at[s, :, own_key],
                kvb.at[s, tile(LOOK, h), pl.ds(a * size, size)],
                kvl_sem.at[s, a],
            )
            cp.start()
            kv_local.append(cp)
    local = [
        pltpu.make_async_copy(g_hbm, gl, loc_sem.at[0]),
        pltpu.make_async_copy(o_hbm, ol, loc_sem.at[1]),
        pltpu.make_async_copy(q_hbm.at[:, :, own_cols], qb.at[:, h], loc_sem.at[2]),
        pltpu.make_async_copy(g_hbm.at[:, :, own_cols], gb.at[:, h], loc_sem.at[3]),
    ]
    for cp in local:
        cp.start()

    for s in range(2):
        for d in range(1, LOOK + 1):
            @pl.when(ids[s] - d < 0)
            def _():
                kvb[s, (LOOK - d) * block:(LOOK - d + 1) * block, :] = jnp.zeros(
                    (block, 2 * size), BF16
                )
    def send(valid, src, dst, send_sem, recv_sem, ctx):
        cp = pltpu.make_async_remote_copy(
            src, dst, send_sem, recv_sem, device_id={"ctx": ctx}, device_id_type=MESH
        )
        pl.when(valid)(cp.start)
        sent.append((valid, cp))

    def spread_part(s, p, i):
        b, src = ids[s], kvb.at[s, tile(LOOK, p), :]
        ctx, half = place(b + 2)
        send(
            b + 2 < n_blocks, src, kvb.at[half, tile(1, p), :],
            kv_send.at[s, 0, i], kv_recv.at[half, 1, p], ctx,
        )
        ctx, half = place(b + 3)
        j = jnp.where(even[s], 2, 0)
        ctx, half = jnp.where(even[s], pair, ctx), jnp.where(even[s], s, half)
        send(
            even[s] | (b + 3 < n_blocks), src, kvb.at[half, tile(j, p), :],
            kv_send.at[s, 1, i], kv_recv.at[half, j, p], ctx,
        )

    def wait_part(s, j, p):
        part = kvb.at[s, tile(j, p), :]
        pl.when(ids[s] - (LOOK - j) >= 0)(
            pltpu.make_async_copy(part, part, kv_recv.at[s, j, p]).wait
        )

    def forward_part(s, p, i):
        wait_part(s, 1, p)
        j = jnp.where(even[s], 0, 2)
        send(
            ids[s] >= 2, kvb.at[s, tile(1, p), :], kvb.at[s, tile(j, p), :],
            kv_send.at[s, 2, i], kv_recv.at[s, j, p], pair,
        )

    @pl.when(h == 0)
    def _():
        count = jnp.int32(1)
        signal(barrier, ctx=pair)
        for ctx in (c - 2, c + 2, c - 3 + 6 * odd):
            inside = (ctx >= 0) & (ctx < n_ctx)
            count = count + inside.astype(jnp.int32)

            @pl.when(inside)
            def _():
                signal(barrier, ctx=ctx)

        pl.semaphore_wait(barrier, count)
        for t in range(1, n_kvh):
            signal(gate.at[1], kvh=t)

    @pl.when(h != 0)
    def _():
        pl.semaphore_wait(gate.at[1], 1)

    for cp in kv_local:
        cp.wait()
    for s in range(2):
        spread_part(s, h, 0)

    local[0].wait()
    local[1].wait()

    def fill_aux(g):
        cols = pl.ds(mult(g * width, width), width)
        for s in range(2):
            prods = gl[s, :, cols].astype(F32) * ol[s, :, cols].astype(F32)
            delta = row_sums(
                jnp.concatenate([prods[:, i * size:(i + 1) * size] for i in range(group)], axis=0), 2
            )
            for k in range(chunks):
                r = 2 * (s * chunks + k)
                aux_s[g, r + 1:r + 2, :] = delta[:1, k * lanes:(k + 1) * lanes]
                lse = lse_ref[s, pl.ds(mult(g * group + k * chunk_heads, chunk_heads), chunk_heads), :]
                for i in range(chunk_heads):
                    aux_s[g, r:r + 1, i * rows:(i + 1) * rows] = lse[i:i + 1]

    for i, t in enumerate(others):
        fill_aux(t)
        cp = pltpu.make_async_remote_copy(
            aux_s.at[t], aux_r.at[h], aux_send_sem.at[i], aux_recv_sem.at[h],
            device_id={"kvh": t}, device_id_type=MESH,
        )
        cp.start()
        auxsent.append(cp)
    for s in range(2):
        for k in range(chunks):
            if s + k:
                send_chunk(s, k)
    for s in range(2):
        for i, t in enumerate(others):
            part = kvb.at[s, tile(LOOK, t), :]
            pltpu.make_async_copy(part, part, kvy_recv.at[s, t]).wait()
            spread_part(s, t, i + 1)
    fill_aux(h)
    aux_r[h] = aux_s[h]

    own_span = slice(LOOK * block, (LOOK + 1) * block)
    ends, total = [], jnp.int32(0)
    for i in range(n_docs):
        total = total + docs_ref[i]
        ends.append(total)
    spot = lax.broadcasted_iota(jnp.int32, (1, lanes), 1) % rows
    key_spot = lax.broadcasted_iota(jnp.int32, (block, lanes), 0)

    def stage(s, slot, dk, dv):
        sb[s, slot, :, :size] = (dk * scale).astype(BF16)
        sb[s, slot, :, size:] = dv.astype(BF16)

    def send_exchange(s, j):
        stage(s, 0, dk_acc[s, tile(j), :], dv_acc[s, tile(j), :])
        send(ids[s] >= 2, sb.at[s, 0], rb.at[s, 2], d_send.at[s, 0], d_recv.at[s, 2], pair)

    def send_direct(s, j):
        stage(s, 1, dk_acc[s, tile(j), :], dv_acc[s, tile(j), :])
        b = ids[s]
        ctx, half = place(b - 3)
        ctx, half = jnp.where(even[s], ctx, pair), jnp.where(even[s], half, s)
        send(
            (~even[s]) | (b - 3 >= 0), sb.at[s, 1], rb.at[half, 1],
            d_send.at[s, 1], d_recv.at[half, 1], ctx,
        )

    def send_combined(s):
        b = ids[s]
        ctx, half = place(b - 2)

        @pl.when(b >= 2)
        def _():
            pltpu.make_async_copy(rb.at[s, 2], rb.at[s, 2], d_recv.at[s, 2]).wait()
            sb[s, 2, :, :size] = (
                dk_acc[s, block:2 * block, :] * scale + rb[s, 2, :, :size].astype(F32)
            ).astype(BF16)
            sb[s, 2, :, size:] = (
                dv_acc[s, block:2 * block, :] + rb[s, 2, :, size:].astype(F32)
            ).astype(BF16)

        send(b >= 2, sb.at[s, 2], rb.at[half, 0], d_send.at[s, 2], d_recv.at[half, 0], ctx)

    def compute(s, p, k, first, last, tiles, dqt=None, finish=True):
        heads = range(k * chunk_heads, (k + 1) * chunk_heads)
        q = jnp.concatenate([qb[s, p, :, n * size:(n + 1) * size] for n in heads], axis=0)
        g = jnp.concatenate([gb[s, p, :, n * size:(n + 1) * size] for n in heads], axis=0)
        r = 2 * (s * chunks + k)
        norm = aux_r[p, r:r + 1, :]
        delta = aux_r[p, r + 1:r + 2, :]
        pos = ids[s] * block + p * rows + spot
        start = jnp.zeros_like(pos)
        for end in ends:
            start = jnp.where(pos >= end, end, start)
        base = (ids[s] - LOOK) * block
        pos, start = pos - base, start - base
        if last:
            tiles = [jnp.where(even[s], 2, 0), jnp.where(even[s], 0, 2), 1, LOOK]
        for i, j in enumerate(tiles):
            span = tile(j)
            st = lax.dot_general(kvb[s, span, :size], q, NT, preferred_element_type=F32)
            t = key_spot + j * block
            allowed = t >= start
            if isinstance(j, int) and j == LOOK:
                allowed = allowed & (t <= pos)
            w = jnp.where(allowed, jnp.exp(st * scale - norm), 0.0)
            dv = jnp.dot(w.astype(BF16), g, preferred_element_type=F32)
            dp = lax.dot_general(kvb[s, span, size:], g, NT, preferred_element_type=F32)
            ds = (w * (dp - delta)).astype(BF16)
            dk = jnp.dot(ds, q, preferred_element_type=F32)
            if first:
                dv_acc[s, span, :] = dv
                dk_acc[s, span, :] = dk
            else:
                dv_acc[s, span, :] += dv
                dk_acc[s, span, :] += dk
            if last and i == 0:
                send_exchange(s, j)
            if last and i == 1:
                send_direct(s, j)
            part = jnp.dot(ktb[s, :, span], ds, preferred_element_type=F32)
            dqt = part if dqt is None else dqt + part
        if last:
            send_combined(s)
        if not finish:
            return dqt
        dq = (jnp.transpose(dqt) * scale).astype(BF16)
        for i, n in enumerate(heads):
            dqo[s, pl.ds(mult(p * rows, rows), rows), n * size:(n + 1) * size] = dq[i * rows:(i + 1) * rows]

    local[2].wait()
    local[3].wait()
    started = {}
    for s in range(2):
        forward_part(s, h, 0)
    for s in range(2):
        ktb[s, :, own_span] = jnp.transpose(kvb[s, own_span, :size])
        for k in range(chunks):
            started[s, k] = compute(s, h, k, k == 0, False, [LOOK], None, False)
        for i, t in enumerate(others):
            forward_part(s, t, i + 1)
    for s in range(2):
        for j in (0, 2):
            for p in range(n_kvh):
                wait_part(s, j, p)
        ktb[s, :, :LOOK * block] = jnp.transpose(kvb[s, :LOOK * block, :size])
        for k in range(chunks):
            compute(s, h, k, k == 0, False, range(LOOK), started[s, k])

    for i, t in enumerate(others):
        pltpu.make_async_copy(aux_r.at[t], aux_r.at[t], aux_recv_sem.at[t]).wait()
    for s in range(2):
        for k in range(chunks):
            for i, t in enumerate(others):
                for a, buf in enumerate((qb, gb)):
                    part = buf.at[s, t, :, pl.ds(k * chunk_heads * size, chunk_heads * size)]
                    pltpu.make_async_copy(part, part, y_recv.at[s, k, t, a]).wait()
                compute(s, t, k, False, k == chunks - 1 and i == n_kvh - 2, range(LOOK + 1))

    for s in range(2):
        own = slice(LOOK * block, (LOOK + 1) * block)
        b = ids[s]
        dk_acc[s, own, :] = dk_acc[s, own, :] * scale
        for slot, valid in ((1, even[s] | (b + 3 < n_blocks)), (0, b + 2 < n_blocks)):
            @pl.when(valid)
            def _():
                pltpu.make_async_copy(rb.at[s, slot], rb.at[s, slot], d_recv.at[s, slot]).wait()
                dk_acc[s, own, :] += rb[s, slot, :, :size].astype(F32)
                dv_acc[s, own, :] += rb[s, slot, :, size:].astype(F32)

        dk_ref[s] = dk_acc[s, own, :].astype(BF16)
        dv_ref[s] = dv_acc[s, own, :].astype(BF16)

    for cp in kvy + ysent + auxsent:
        cp.wait_send()
    for valid, cp in sent:
        pl.when(valid)(cp.wait_send)


def write_out(*refs):
    copies = [
        pltpu.make_async_copy(refs[i], refs[3 + i], refs[6].at[i]) for i in range(3)
    ]
    for cp in copies:
        cp.start()
    for cp in copies:
        cp.wait()


def body(
    doc_lengths,
    queries,
    key_matrix,
    value_matrix,
    forward_output,
    output_cotangent,
    log_normalizer_rows,
):
    n_ctx, n_kvh = lax.axis_size("ctx"), lax.axis_size("kvh")
    rows = queries.shape[1]
    group = queries.shape[2] // key_matrix.shape[2]
    size = key_matrix.shape[2] // n_kvh
    block = rows * n_kvh
    width = group * size
    chunk_heads = max(1, min(group, 256 // rows))
    chunks = group // chunk_heads
    dims = (n_ctx, n_kvh, rows, group, size, chunk_heads, doc_lengths.shape[0])
    peers = n_kvh - 1
    lanes = chunk_heads * rows
    aux_rows = -(-4 * chunks // 8) * 8
    dma = pltpu.SemaphoreType.DMA
    anywhere = pl.BlockSpec(memory_space=pl.ANY)
    vmem = pl.BlockSpec(memory_space=pltpu.VMEM)
    grads = pl.pallas_call(
        functools.partial(kernel, dims),
        out_shape=(
            pltpu.VMEM((2, block, width), BF16),
            pltpu.VMEM((2, block, size), BF16),
            pltpu.VMEM((2, block, size), BF16),
        ),
        in_specs=[pl.BlockSpec(memory_space=pltpu.SMEM), vmem] + [anywhere] * 5,
        out_specs=(vmem, vmem, vmem),
        scratch_shapes=[
            pltpu.VMEM((2, n_kvh, rows, width), BF16),
            pltpu.VMEM((2, n_kvh, rows, width), BF16),
            pltpu.VMEM((2, rows, width * n_kvh), BF16),
            pltpu.VMEM((2, rows, width * n_kvh), BF16),
            pltpu.VMEM((2, (LOOK + 1) * block, 2 * size), BF16),
            pltpu.VMEM((2, size, (LOOK + 1) * block), BF16),
            pltpu.VMEM((2, (LOOK + 1) * block, size), F32),
            pltpu.VMEM((2, (LOOK + 1) * block, size), F32),
            pltpu.VMEM((2, 3, block, 2 * size), BF16),
            pltpu.VMEM((2, 3, block, 2 * size), BF16),
            pltpu.VMEM((n_kvh, aux_rows, lanes), F32),
            pltpu.VMEM((n_kvh, aux_rows, lanes), F32),
            dma((4,)),
            dma((2, 2)),
            dma((2, chunks, peers, 2)),
            dma((2, chunks, n_kvh, 2)),
            dma((2, peers, 2)),
            dma((2, n_kvh)),
            dma((2, 3, n_kvh)),
            dma((2, LOOK, n_kvh)),
            dma((peers,)),
            dma((n_kvh,)),
            dma((2, 3)),
            dma((2, 3)),
            pltpu.SemaphoreType.REGULAR((2,)),
        ],
        compiler_params=pltpu.CompilerParams(collective_id=0, has_side_effects=True),
    )(
        doc_lengths, jnp.transpose(log_normalizer_rows, (0, 2, 1)), queries, key_matrix, value_matrix,
        forward_output, output_cotangent,
    )
    return pl.pallas_call(
        write_out,
        out_shape=tuple(jax.ShapeDtypeStruct(x.shape, x.dtype) for x in grads),
        in_specs=[vmem] * 3,
        out_specs=[anywhere] * 3,
        scratch_shapes=[dma((3,))],
    )(*[pltpu.with_memory_space_constraint(x, pltpu.VMEM) for x in grads])


def solution(mesh):
    rows = P(None, ("ctx", "kvh"), None)
    return jax.shard_map(
        body,
        mesh=mesh,
        in_specs=(P(),) + (rows,) * 6,
        out_specs=(P(None, "ctx", "kvh"),) * 3,
        check_vma=False,
    )
```

```python
import functools

import jax
import jax.numpy as jnp
from jax import lax
from jax.experimental import pallas as pl
from jax.experimental.pallas import tpu as pltpu
from jax.sharding import PartitionSpec as P

LOOK = 3
MESH = pl.DeviceIdType.MESH
F32 = jnp.float32
BF16 = jnp.bfloat16
NT = (((1,), (1,)), ((), ()))


def row_sums(values, terms):
    ones = jnp.ones((8, values.shape[1]), BF16)
    total, rest = None, values
    for _ in range(terms):
        part = rest.astype(BF16)
        rest = rest - part.astype(F32)
        term = lax.dot_general(ones, part, NT, preferred_element_type=F32)
        total = term if total is None else total + term
    return total


def kernel(
    dims,
    docs_ref, lse_ref, q_hbm, k_hbm, v_hbm, o_hbm, g_hbm,
    dqo, dk_ref, dv_ref,
    qb, gb, gl, ol, kvb, ktb, dk_acc, dv_acc, sb, rb, aux_s, aux_r,
    loc_sem, kvl_sem, y_send, y_recv, kvy_send, kvy_recv, kv_send, kv_recv,
    aux_send_sem, aux_recv_sem, d_send, d_recv, gate,
):
    n_ctx, n_kvh, rows, group, size, chunk_heads, n_docs = dims
    block = n_kvh * rows
    width = group * size
    chunks = group // chunk_heads
    lanes = chunk_heads * rows
    n_blocks = 2 * n_ctx
    scale = size ** -0.5
    c = lax.axis_index("ctx")
    h = lax.axis_index("kvh")
    ids = (c, n_blocks - 1 - c)
    odd = lax.rem(c, 2)
    pair = c + 1 - 2 * odd
    even = (odd == 0, odd == 1)
    others = [lax.rem(h + i, n_kvh) for i in range(1, n_kvh)]

    def place(b):
        return jnp.where(b < n_ctx, b, n_blocks - 1 - b), jnp.where(b < n_ctx, 0, 1)

    def mult(x, m):
        return pl.multiple_of(x, m)

    def tile(j, p=None):
        if p is None:
            return pl.ds(mult(j * block, block), block)
        return pl.ds(mult(j * block + p * rows, rows), rows)

    barrier = pltpu.get_barrier_semaphore()
    leader = n_kvh - 1

    def signal(sem, **device):
        pl.semaphore_signal(sem, inc=1, device_id=device, device_id_type=MESH)

    @pl.when(h != leader)
    def _():
        signal(barrier, kvh=leader)

    @pl.when(h == leader)
    def _():
        if leader:
            pl.semaphore_wait(barrier, leader)
        for t in range(leader):
            signal(gate.at[0], kvh=t)

    @pl.when(h != leader)
    def _():
        pl.semaphore_wait(gate.at[0], 1)

    kvy, ysent, auxsent, sent = [], [], [], []
    for s in range(2):
        for i, t in enumerate(others):
            for a, src in enumerate((k_hbm, v_hbm)):
                cp = pltpu.make_async_remote_copy(
                    src.at[s, :, pl.ds(mult(t * size, size), size)],
                    kvb.at[s, tile(LOOK, h), pl.ds(a * size, size)],
                    kvy_send.at[s, i, a],
                    kvy_recv.at[s, h],
                    device_id={"kvh": t},
                    device_id_type=MESH,
                )
                cp.start()
                kvy.append(cp)

    def send_chunk(s, k):
        for i, t in enumerate(others):
            for a, (src, dst) in enumerate(((q_hbm, qb), (g_hbm, gb))):
                span = chunk_heads * size
                cp = pltpu.make_async_remote_copy(
                    src.at[s, :, pl.ds(mult(t * width + k * span, span), span)],
                    dst.at[s, h, :, pl.ds(k * span, span)],
                    y_send.at[s, k, i, a],
                    y_recv.at[s, k, h, a],
                    device_id={"kvh": t},
                    device_id_type=MESH,
                )
                cp.start()
                ysent.append(cp)

    send_chunk(0, 0)
    own_cols = pl.ds(mult(h * width, width), width)
    own_key = pl.ds(mult(h * size, size), size)
    kv_local = []
    for s in range(2):
        for a, src in enumerate((k_hbm, v_hbm)):
            cp = pltpu.make_async_copy(
                src.at[s, :, own_key],
                kvb.at[s, tile(LOOK, h), pl.ds(a * size, size)],
                kvl_sem.at[s, a],
            )
            cp.start()
            kv_local.append(cp)
    local = [
        pltpu.make_async_copy(g_hbm, gl, loc_sem.at[0]),
        pltpu.make_async_copy(o_hbm, ol, loc_sem.at[1]),
        pltpu.make_async_copy(q_hbm.at[:, :, own_cols], qb.at[:, h], loc_sem.at[2]),
        pltpu.make_async_copy(g_hbm.at[:, :, own_cols], gb.at[:, h], loc_sem.at[3]),
    ]
    for cp in local:
        cp.start()

    for s in range(2):
        for d in range(1, LOOK + 1):
            @pl.when(ids[s] - d < 0)
            def _():
                kvb[s, (LOOK - d) * block:(LOOK - d + 1) * block, :] = jnp.zeros(
                    (block, 2 * size), BF16
                )
    def send(valid, src, dst, send_sem, recv_sem, ctx):
        cp = pltpu.make_async_remote_copy(
            src, dst, send_sem, recv_sem, device_id={"ctx": ctx}, device_id_type=MESH
        )
        pl.when(valid)(cp.start)
        sent.append((valid, cp))

    def spread_part(s, p, i):
        b, src = ids[s], kvb.at[s, tile(LOOK, p), :]
        ctx, half = place(b + 2)
        send(
            b + 2 < n_blocks, src, kvb.at[half, tile(1, p), :],
            kv_send.at[s, 0, i], kv_recv.at[half, 1, p], ctx,
        )
        ctx, half = place(b + 3)
        j = jnp.where(even[s], 2, 0)
        ctx, half = jnp.where(even[s], pair, ctx), jnp.where(even[s], s, half)
        send(
            even[s] | (b + 3 < n_blocks), src, kvb.at[half, tile(j, p), :],
            kv_send.at[s, 1, i], kv_recv.at[half, j, p], ctx,
        )

    def wait_part(s, j, p):
        part = kvb.at[s, tile(j, p), :]
        pl.when(ids[s] - (LOOK - j) >= 0)(
            pltpu.make_async_copy(part, part, kv_recv.at[s, j, p]).wait
        )

    def forward_part(s, p, i):
        wait_part(s, 1, p)
        j = jnp.where(even[s], 0, 2)
        send(
            ids[s] >= 2, kvb.at[s, tile(1, p), :], kvb.at[s, tile(j, p), :],
            kv_send.at[s, 2, i], kv_recv.at[s, j, p], pair,
        )

    @pl.when(h == 0)
    def _():
        count = jnp.int32(1)
        signal(barrier, ctx=pair)
        for ctx in (c - 2, c + 2, c - 3 + 6 * odd):
            inside = (ctx >= 0) & (ctx < n_ctx)
            count = count + inside.astype(jnp.int32)

            @pl.when(inside)
            def _():
                signal(barrier, ctx=ctx)

        pl.semaphore_wait(barrier, count)
        for t in range(1, n_kvh):
            signal(gate.at[1], kvh=t)

    @pl.when(h != 0)
    def _():
        pl.semaphore_wait(gate.at[1], 1)

    for cp in kv_local:
        cp.wait()
    for s in range(2):
        spread_part(s, h, 0)

    local[0].wait()
    local[1].wait()

    def fill_aux(g):
        cols = pl.ds(mult(g * width, width), width)
        for s in range(2):
            prods = gl[s, :, cols].astype(F32) * ol[s, :, cols].astype(F32)
            delta = row_sums(
                jnp.concatenate([prods[:, i * size:(i + 1) * size] for i in range(group)], axis=0), 2
            )
            for k in range(chunks):
                r = 2 * (s * chunks + k)
                aux_s[g, r + 1:r + 2, :] = delta[:1, k * lanes:(k + 1) * lanes]
                lse = lse_ref[s, pl.ds(mult(g * group + k * chunk_heads, chunk_heads), chunk_heads), :]
                for i in range(chunk_heads):
                    aux_s[g, r:r + 1, i * rows:(i + 1) * rows] = lse[i:i + 1]

    for i, t in enumerate(others):
        fill_aux(t)
        cp = pltpu.make_async_remote_copy(
            aux_s.at[t], aux_r.at[h], aux_send_sem.at[i], aux_recv_sem.at[h],
            device_id={"kvh": t}, device_id_type=MESH,
        )
        cp.start()
        auxsent.append(cp)
    for s in range(2):
        for k in range(chunks):
            if s + k:
                send_chunk(s, k)
    for s in range(2):
        for i, t in enumerate(others):
            part = kvb.at[s, tile(LOOK, t), :]
            pltpu.make_async_copy(part, part, kvy_recv.at[s, t]).wait()
            spread_part(s, t, i + 1)
    fill_aux(h)
    aux_r[h] = aux_s[h]

    own_span = slice(LOOK * block, (LOOK + 1) * block)
    ends, total = [], jnp.int32(0)
    for i in range(n_docs):
        total = total + docs_ref[i]
        ends.append(total)
    spot = lax.broadcasted_iota(jnp.int32, (1, lanes), 1) % rows
    key_spot = lax.broadcasted_iota(jnp.int32, (block, lanes), 0)

    def stage(s, slot, dk, dv):
        sb[s, slot, :, :size] = (dk * scale).astype(BF16)
        sb[s, slot, :, size:] = dv.astype(BF16)

    def send_exchange(s, j):
        stage(s, 0, dk_acc[s, tile(j), :], dv_acc[s, tile(j), :])
        send(ids[s] >= 2, sb.at[s, 0], rb.at[s, 2], d_send.at[s, 0], d_recv.at[s, 2], pair)

    def send_direct(s, j):
        stage(s, 1, dk_acc[s, tile(j), :], dv_acc[s, tile(j), :])
        b = ids[s]
        ctx, half = place(b - 3)
        ctx, half = jnp.where(even[s], ctx, pair), jnp.where(even[s], half, s)
        send(
            (~even[s]) | (b - 3 >= 0), sb.at[s, 1], rb.at[half, 1],
            d_send.at[s, 1], d_recv.at[half, 1], ctx,
        )

    def send_combined(s):
        b = ids[s]
        ctx, half = place(b - 2)

        @pl.when(b >= 2)
        def _():
            pltpu.make_async_copy(rb.at[s, 2], rb.at[s, 2], d_recv.at[s, 2]).wait()
            sb[s, 2, :, :size] = (
                dk_acc[s, block:2 * block, :] * scale + rb[s, 2, :, :size].astype(F32)
            ).astype(BF16)
            sb[s, 2, :, size:] = (
                dv_acc[s, block:2 * block, :] + rb[s, 2, :, size:].astype(F32)
            ).astype(BF16)

        send(b >= 2, sb.at[s, 2], rb.at[half, 0], d_send.at[s, 2], d_recv.at[half, 0], ctx)

    def compute(s, p, k, first, last, tiles, dqt=None, finish=True):
        heads = range(k * chunk_heads, (k + 1) * chunk_heads)
        q = jnp.concatenate([qb[s, p, :, n * size:(n + 1) * size] for n in heads], axis=0)
        g = jnp.concatenate([gb[s, p, :, n * size:(n + 1) * size] for n in heads], axis=0)
        r = 2 * (s * chunks + k)
        norm = aux_r[p, r:r + 1, :]
        delta = aux_r[p, r + 1:r + 2, :]
        pos = ids[s] * block + p * rows + spot
        start = jnp.zeros_like(pos)
        for end in ends:
            start = jnp.where(pos >= end, end, start)
        base = (ids[s] - LOOK) * block
        pos, start = pos - base, start - base
        if last:
            tiles = [jnp.where(even[s], 2, 0), jnp.where(even[s], 0, 2), 1, LOOK]
        lo, hi = (tiles[0], tiles[-1]) if not last else (0, LOOK)
        span = slice(lo * block, (hi + 1) * block)
        size_k = (hi + 1 - lo) * block
        st = lax.dot_general(kvb[s, span, :size], q, NT, preferred_element_type=F32)
        t = lax.broadcasted_iota(jnp.int32, (size_k, lanes), 0) + lo * block
        allowed = t >= start
        if hi == LOOK:
            allowed = allowed & (t <= pos)
        w = jnp.where(allowed, jnp.exp(st * scale - norm), 0.0)
        dv = jnp.dot(w.astype(BF16), g, preferred_element_type=F32)
        dp = lax.dot_general(kvb[s, span, size:], g, NT, preferred_element_type=F32)
        ds = (w * (dp - delta)).astype(BF16)
        dk = jnp.dot(ds, q, preferred_element_type=F32)
        if first:
            dv_acc[s, span, :] = dv
            dk_acc[s, span, :] = dk
        else:
            dv_acc[s, span, :] += dv
            dk_acc[s, span, :] += dk
        part = jnp.dot(ktb[s, :, span], ds, preferred_element_type=F32)
        dqt = part if dqt is None else dqt + part
        if last:
            send_exchange(s, jnp.where(even[s], 2, 0))
            send_direct(s, jnp.where(even[s], 0, 2))
        if last:
            send_combined(s)
        if not finish:
            return dqt
        dq = (jnp.transpose(dqt) * scale).astype(BF16)
        for i, n in enumerate(heads):
            dqo[s, pl.ds(mult(p * rows, rows), rows), n * size:(n + 1) * size] = dq[i * rows:(i + 1) * rows]

    local[2].wait()
    local[3].wait()
    started = {}
    for s in range(2):
        forward_part(s, h, 0)
    for s in range(2):
        ktb[s, :, own_span] = jnp.transpose(kvb[s, own_span, :size])
        for k in range(chunks):
            started[s, k] = compute(s, h, k, k == 0, False, [LOOK], None, False)
        for i, t in enumerate(others):
            forward_part(s, t, i + 1)
    for s in range(2):
        for j in (0, 2):
            for p in range(n_kvh):
                wait_part(s, j, p)
        ktb[s, :, :LOOK * block] = jnp.transpose(kvb[s, :LOOK * block, :size])
        for k in range(chunks):
            compute(s, h, k, k == 0, False, range(LOOK), started[s, k])

    for i, t in enumerate(others):
        pltpu.make_async_copy(aux_r.at[t], aux_r.at[t], aux_recv_sem.at[t]).wait()
    for s in range(2):
        for k in range(chunks):
            for i, t in enumerate(others):
                for a, buf in enumerate((qb, gb)):
                    part = buf.at[s, t, :, pl.ds(k * chunk_heads * size, chunk_heads * size)]
                    pltpu.make_async_copy(part, part, y_recv.at[s, k, t, a]).wait()
                compute(s, t, k, False, k == chunks - 1 and i == n_kvh - 2, range(LOOK + 1))

    for s in range(2):
        own = slice(LOOK * block, (LOOK + 1) * block)
        b = ids[s]
        dk_acc[s, own, :] = dk_acc[s, own, :] * scale
        for slot, valid in ((1, even[s] | (b + 3 < n_blocks)), (0, b + 2 < n_blocks)):
            @pl.when(valid)
            def _():
                pltpu.make_async_copy(rb.at[s, slot], rb.at[s, slot], d_recv.at[s, slot]).wait()
                dk_acc[s, own, :] += rb[s, slot, :, :size].astype(F32)
                dv_acc[s, own, :] += rb[s, slot, :, size:].astype(F32)

        dk_ref[s] = dk_acc[s, own, :].astype(BF16)
        dv_ref[s] = dv_acc[s, own, :].astype(BF16)

    for cp in kvy + ysent + auxsent:
        cp.wait_send()
    for valid, cp in sent:
        pl.when(valid)(cp.wait_send)


def write_out(*refs):
    copies = [
        pltpu.make_async_copy(refs[i], refs[3 + i], refs[6].at[i]) for i in range(3)
    ]
    for cp in copies:
        cp.start()
    for cp in copies:
        cp.wait()


def body(
    doc_lengths,
    queries,
    key_matrix,
    value_matrix,
    forward_output,
    output_cotangent,
    log_normalizer_rows,
):
    n_ctx, n_kvh = lax.axis_size("ctx"), lax.axis_size("kvh")
    rows = queries.shape[1]
    group = queries.shape[2] // key_matrix.shape[2]
    size = key_matrix.shape[2] // n_kvh
    block = rows * n_kvh
    width = group * size
    chunk_heads = max(1, min(group, 256 // rows))
    chunks = group // chunk_heads
    dims = (n_ctx, n_kvh, rows, group, size, chunk_heads, doc_lengths.shape[0])
    peers = n_kvh - 1
    lanes = chunk_heads * rows
    aux_rows = -(-4 * chunks // 8) * 8
    dma = pltpu.SemaphoreType.DMA
    anywhere = pl.BlockSpec(memory_space=pl.ANY)
    vmem = pl.BlockSpec(memory_space=pltpu.VMEM)
    grads = pl.pallas_call(
        functools.partial(kernel, dims),
        out_shape=(
            pltpu.VMEM((2, block, width), BF16),
            pltpu.VMEM((2, block, size), BF16),
            pltpu.VMEM((2, block, size), BF16),
        ),
        in_specs=[pl.BlockSpec(memory_space=pltpu.SMEM), vmem] + [anywhere] * 5,
        out_specs=(vmem, vmem, vmem),
        scratch_shapes=[
            pltpu.VMEM((2, n_kvh, rows, width), BF16),
            pltpu.VMEM((2, n_kvh, rows, width), BF16),
            pltpu.VMEM((2, rows, width * n_kvh), BF16),
            pltpu.VMEM((2, rows, width * n_kvh), BF16),
            pltpu.VMEM((2, (LOOK + 1) * block, 2 * size), BF16),
            pltpu.VMEM((2, size, (LOOK + 1) * block), BF16),
            pltpu.VMEM((2, (LOOK + 1) * block, size), F32),
            pltpu.VMEM((2, (LOOK + 1) * block, size), F32),
            pltpu.VMEM((2, 3, block, 2 * size), BF16),
            pltpu.VMEM((2, 3, block, 2 * size), BF16),
            pltpu.VMEM((n_kvh, aux_rows, lanes), F32),
            pltpu.VMEM((n_kvh, aux_rows, lanes), F32),
            dma((4,)),
            dma((2, 2)),
            dma((2, chunks, peers, 2)),
            dma((2, chunks, n_kvh, 2)),
            dma((2, peers, 2)),
            dma((2, n_kvh)),
            dma((2, 3, n_kvh)),
            dma((2, LOOK, n_kvh)),
            dma((peers,)),
            dma((n_kvh,)),
            dma((2, 3)),
            dma((2, 3)),
            pltpu.SemaphoreType.REGULAR((2,)),
        ],
        compiler_params=pltpu.CompilerParams(collective_id=0, has_side_effects=True),
    )(
        doc_lengths, jnp.transpose(log_normalizer_rows, (0, 2, 1)), queries, key_matrix, value_matrix,
        forward_output, output_cotangent,
    )
    return pl.pallas_call(
        write_out,
        out_shape=tuple(jax.ShapeDtypeStruct(x.shape, x.dtype) for x in grads),
        in_specs=[vmem] * 3,
        out_specs=[anywhere] * 3,
        scratch_shapes=[dma((3,))],
    )(*[pltpu.with_memory_space_constraint(x, pltpu.VMEM) for x in grads])


def solution(mesh):
    rows = P(None, ("ctx", "kvh"), None)
    return jax.shard_map(
        body,
        mesh=mesh,
        in_specs=(P(),) + (rows,) * 6,
        out_specs=(P(None, "ctx", "kvh"),) * 3,
        check_vma=False,
    )
```

```python
import functools

import jax
import jax.numpy as jnp
from jax import lax
from jax.experimental import pallas as pl
from jax.experimental.pallas import tpu as pltpu
from jax.sharding import PartitionSpec as P

LOOK = 3
MESH = pl.DeviceIdType.MESH
F32 = jnp.float32
BF16 = jnp.bfloat16
NT = (((1,), (1,)), ((), ()))


def row_sums(values, terms):
    ones = jnp.ones((8, values.shape[1]), BF16)
    total, rest = None, values
    for _ in range(terms):
        part = rest.astype(BF16)
        rest = rest - part.astype(F32)
        term = lax.dot_general(ones, part, NT, preferred_element_type=F32)
        total = term if total is None else total + term
    return total


def kernel(
    dims,
    docs_hbm, lse_hbm, q_hbm, k_hbm, v_hbm, o_hbm, g_hbm,
    dqo, dk_ref, dv_ref,
    docs_ref, lse_ref, qb, gb, gl, ol, kvb, ktb, dk_acc, dv_acc, sb, rb, aux_s, aux_r,
    loc_sem, kvl_sem, y_send, y_recv, kvy_send, kvy_recv, kv_send, kv_recv,
    aux_send_sem, aux_recv_sem, d_send, d_recv, gate,
):
    n_ctx, n_kvh, rows, group, size, chunk_heads, n_docs = dims
    block = n_kvh * rows
    width = group * size
    chunks = group // chunk_heads
    lanes = chunk_heads * rows
    n_blocks = 2 * n_ctx
    scale = size ** -0.5
    c = lax.axis_index("ctx")
    h = lax.axis_index("kvh")
    ids = (c, n_blocks - 1 - c)
    odd = lax.rem(c, 2)
    pair = c + 1 - 2 * odd
    even = (odd == 0, odd == 1)
    others = [lax.rem(h + i, n_kvh) for i in range(1, n_kvh)]

    def place(b):
        return jnp.where(b < n_ctx, b, n_blocks - 1 - b), jnp.where(b < n_ctx, 0, 1)

    def mult(x, m):
        return pl.multiple_of(x, m)

    def tile(j, p=None):
        if p is None:
            return pl.ds(mult(j * block, block), block)
        return pl.ds(mult(j * block + p * rows, rows), rows)

    barrier = pltpu.get_barrier_semaphore()
    leader = n_kvh - 1

    def signal(sem, **device):
        pl.semaphore_signal(sem, inc=1, device_id=device, device_id_type=MESH)

    @pl.when(h != leader)
    def _():
        signal(barrier, kvh=leader)

    @pl.when(h == leader)
    def _():
        if leader:
            pl.semaphore_wait(barrier, leader)
        for t in range(leader):
            signal(gate.at[0], kvh=t)

    @pl.when(h != leader)
    def _():
        pl.semaphore_wait(gate.at[0], 1)

    kvy, ysent, auxsent, sent = [], [], [], []
    for s in range(2):
        for i, t in enumerate(others):
            for a, src in enumerate((k_hbm, v_hbm)):
                cp = pltpu.make_async_remote_copy(
                    src.at[s, :, pl.ds(mult(t * size, size), size)],
                    kvb.at[s, tile(LOOK, h), pl.ds(a * size, size)],
                    kvy_send.at[s, i, a],
                    kvy_recv.at[s, h],
                    device_id={"kvh": t},
                    device_id_type=MESH,
                )
                cp.start()
                kvy.append(cp)

    def send_chunk(s, k):
        for i, t in enumerate(others):
            for a, (src, dst) in enumerate(((q_hbm, qb), (g_hbm, gb))):
                span = chunk_heads * size
                cp = pltpu.make_async_remote_copy(
                    src.at[s, :, pl.ds(mult(t * width + k * span, span), span)],
                    dst.at[s, h, :, pl.ds(k * span, span)],
                    y_send.at[s, k, i, a],
                    y_recv.at[s, k, h, a],
                    device_id={"kvh": t},
                    device_id_type=MESH,
                )
                cp.start()
                ysent.append(cp)

    send_chunk(0, 0)
    own_cols = pl.ds(mult(h * width, width), width)
    own_key = pl.ds(mult(h * size, size), size)
    kv_local = []
    for s in range(2):
        for a, src in enumerate((k_hbm, v_hbm)):
            cp = pltpu.make_async_copy(
                src.at[s, :, own_key],
                kvb.at[s, tile(LOOK, h), pl.ds(a * size, size)],
                kvl_sem.at[s, a],
            )
            cp.start()
            kv_local.append(cp)
    local = [
        pltpu.make_async_copy(g_hbm, gl, loc_sem.at[0]),
        pltpu.make_async_copy(o_hbm, ol, loc_sem.at[1]),
        pltpu.make_async_copy(q_hbm.at[:, :, own_cols], qb.at[:, h], loc_sem.at[2]),
        pltpu.make_async_copy(g_hbm.at[:, :, own_cols], gb.at[:, h], loc_sem.at[3]),
        pltpu.make_async_copy(lse_hbm, lse_ref, loc_sem.at[4]),
        pltpu.make_async_copy(docs_hbm, docs_ref, loc_sem.at[5]),
    ]
    for cp in local:
        cp.start()

    for s in range(2):
        for d in range(1, LOOK + 1):
            @pl.when(ids[s] - d < 0)
            def _():
                kvb[s, (LOOK - d) * block:(LOOK - d + 1) * block, :] = jnp.zeros(
                    (block, 2 * size), BF16
                )
    def send(valid, src, dst, send_sem, recv_sem, ctx):
        cp = pltpu.make_async_remote_copy(
            src, dst, send_sem, recv_sem, device_id={"ctx": ctx}, device_id_type=MESH
        )
        pl.when(valid)(cp.start)
        sent.append((valid, cp))

    def spread_part(s, p, i):
        b, src = ids[s], kvb.at[s, tile(LOOK, p), :]
        ctx, half = place(b + 2)
        send(
            b + 2 < n_blocks, src, kvb.at[half, tile(1, p), :],
            kv_send.at[s, 0, i], kv_recv.at[half, 1, p], ctx,
        )
        ctx, half = place(b + 3)
        j = jnp.where(even[s], 2, 0)
        ctx, half = jnp.where(even[s], pair, ctx), jnp.where(even[s], s, half)
        send(
            even[s] | (b + 3 < n_blocks), src, kvb.at[half, tile(j, p), :],
            kv_send.at[s, 1, i], kv_recv.at[half, j, p], ctx,
        )

    def wait_part(s, j, p):
        part = kvb.at[s, tile(j, p), :]
        pl.when(ids[s] - (LOOK - j) >= 0)(
            pltpu.make_async_copy(part, part, kv_recv.at[s, j, p]).wait
        )

    def forward_part(s, p, i):
        wait_part(s, 1, p)
        j = jnp.where(even[s], 0, 2)
        send(
            ids[s] >= 2, kvb.at[s, tile(1, p), :], kvb.at[s, tile(j, p), :],
            kv_send.at[s, 2, i], kv_recv.at[s, j, p], pair,
        )

    @pl.when(h == 0)
    def _():
        count = jnp.int32(1)
        signal(barrier, ctx=pair)
        for ctx in (c - 2, c + 2, c - 3 + 6 * odd):
            inside = (ctx >= 0) & (ctx < n_ctx)
            count = count + inside.astype(jnp.int32)

            @pl.when(inside)
            def _():
                signal(barrier, ctx=ctx)

        pl.semaphore_wait(barrier, count)
        for t in range(1, n_kvh):
            signal(gate.at[1], kvh=t)

    @pl.when(h != 0)
    def _():
        pl.semaphore_wait(gate.at[1], 1)

    for cp in kv_local:
        cp.wait()
    for s in range(2):
        spread_part(s, h, 0)

    local[0].wait()
    local[1].wait()
    local[4].wait()

    def fill_aux(g):
        cols = pl.ds(mult(g * width, width), width)
        for s in range(2):
            prods = gl[s, :, cols].astype(F32) * ol[s, :, cols].astype(F32)
            delta = row_sums(
                jnp.concatenate([prods[:, i * size:(i + 1) * size] for i in range(group)], axis=0), 2
            )
            for k in range(chunks):
                r = 2 * (s * chunks + k)
                aux_s[g, r + 1:r + 2, :] = delta[:1, k * lanes:(k + 1) * lanes]
                lse = lse_ref[s, pl.ds(mult(g * group + k * chunk_heads, chunk_heads), chunk_heads), :]
                for i in range(chunk_heads):
                    aux_s[g, r:r + 1, i * rows:(i + 1) * rows] = lse[i:i + 1]

    for i, t in enumerate(others):
        fill_aux(t)
        cp = pltpu.make_async_remote_copy(
            aux_s.at[t], aux_r.at[h], aux_send_sem.at[i], aux_recv_sem.at[h],
            device_id={"kvh": t}, device_id_type=MESH,
        )
        cp.start()
        auxsent.append(cp)
    for s in range(2):
        for k in range(chunks):
            if s + k:
                send_chunk(s, k)
    for s in range(2):
        for i, t in enumerate(others):
            part = kvb.at[s, tile(LOOK, t), :]
            pltpu.make_async_copy(part, part, kvy_recv.at[s, t]).wait()
            spread_part(s, t, i + 1)
    fill_aux(h)
    aux_r[h] = aux_s[h]

    own_span = slice(LOOK * block, (LOOK + 1) * block)
    local[5].wait()
    ends, total = [], jnp.int32(0)
    for i in range(n_docs):
        total = total + docs_ref[i]
        ends.append(total)
    spot = lax.broadcasted_iota(jnp.int32, (1, lanes), 1) % rows
    key_spot = lax.broadcasted_iota(jnp.int32, (block, lanes), 0)

    def stage(s, slot, dk, dv):
        sb[s, slot, :, :size] = (dk * scale).astype(BF16)
        sb[s, slot, :, size:] = dv.astype(BF16)

    def send_exchange(s, j):
        stage(s, 0, dk_acc[s, tile(j), :], dv_acc[s, tile(j), :])
        send(ids[s] >= 2, sb.at[s, 0], rb.at[s, 2], d_send.at[s, 0], d_recv.at[s, 2], pair)

    def send_direct(s, j):
        stage(s, 1, dk_acc[s, tile(j), :], dv_acc[s, tile(j), :])
        b = ids[s]
        ctx, half = place(b - 3)
        ctx, half = jnp.where(even[s], ctx, pair), jnp.where(even[s], half, s)
        send(
            (~even[s]) | (b - 3 >= 0), sb.at[s, 1], rb.at[half, 1],
            d_send.at[s, 1], d_recv.at[half, 1], ctx,
        )

    def send_combined(s):
        b = ids[s]
        ctx, half = place(b - 2)

        @pl.when(b >= 2)
        def _():
            pltpu.make_async_copy(rb.at[s, 2], rb.at[s, 2], d_recv.at[s, 2]).wait()
            sb[s, 2, :, :size] = (
                dk_acc[s, block:2 * block, :] * scale + rb[s, 2, :, :size].astype(F32)
            ).astype(BF16)
            sb[s, 2, :, size:] = (
                dv_acc[s, block:2 * block, :] + rb[s, 2, :, size:].astype(F32)
            ).astype(BF16)

        send(b >= 2, sb.at[s, 2], rb.at[half, 0], d_send.at[s, 2], d_recv.at[half, 0], ctx)

    def compute(s, p, k, first, last, tiles, dqt=None, finish=True):
        heads = range(k * chunk_heads, (k + 1) * chunk_heads)
        q = jnp.concatenate([qb[s, p, :, n * size:(n + 1) * size] for n in heads], axis=0)
        g = jnp.concatenate([gb[s, p, :, n * size:(n + 1) * size] for n in heads], axis=0)
        r = 2 * (s * chunks + k)
        norm = aux_r[p, r:r + 1, :]
        delta = aux_r[p, r + 1:r + 2, :]
        pos = ids[s] * block + p * rows + spot
        start = jnp.zeros_like(pos)
        for end in ends:
            start = jnp.where(pos >= end, end, start)
        base = (ids[s] - LOOK) * block
        pos, start = pos - base, start - base
        if last:
            tiles = [jnp.where(even[s], 2, 0), jnp.where(even[s], 0, 2), 1, LOOK]
        lo, hi = (tiles[0], tiles[-1]) if not last else (0, LOOK)
        span = slice(lo * block, (hi + 1) * block)
        size_k = (hi + 1 - lo) * block
        st = lax.dot_general(kvb[s, span, :size], q, NT, preferred_element_type=F32)
        t = lax.broadcasted_iota(jnp.int32, (size_k, lanes), 0) + lo * block
        allowed = t >= start
        if hi == LOOK:
            allowed = allowed & (t <= pos)
        w = jnp.where(allowed, jnp.exp(st * scale - norm), 0.0)
        dv = jnp.dot(w.astype(BF16), g, preferred_element_type=F32)
        dp = lax.dot_general(kvb[s, span, size:], g, NT, preferred_element_type=F32)
        ds = (w * (dp - delta)).astype(BF16)
        dk = jnp.dot(ds, q, preferred_element_type=F32)
        if first:
            dv_acc[s, span, :] = dv
            dk_acc[s, span, :] = dk
        else:
            dv_acc[s, span, :] += dv
            dk_acc[s, span, :] += dk
        part = jnp.dot(ktb[s, :, span], ds, preferred_element_type=F32)
        dqt = part if dqt is None else dqt + part
        if last:
            send_exchange(s, jnp.where(even[s], 2, 0))
            send_direct(s, jnp.where(even[s], 0, 2))
        if last:
            send_combined(s)
        if not finish:
            return dqt
        dq = (jnp.transpose(dqt) * scale).astype(BF16)
        for i, n in enumerate(heads):
            dqo[s, pl.ds(mult(p * rows, rows), rows), n * size:(n + 1) * size] = dq[i * rows:(i + 1) * rows]

    local[2].wait()
    local[3].wait()
    started = {}
    for s in range(2):
        forward_part(s, h, 0)
    for s in range(2):
        ktb[s, :, own_span] = jnp.transpose(kvb[s, own_span, :size])
        for k in range(chunks):
            started[s, k] = compute(s, h, k, k == 0, False, [LOOK], None, False)
        for i, t in enumerate(others):
            forward_part(s, t, i + 1)
    for s in range(2):
        for j in (0, 2):
            for p in range(n_kvh):
                wait_part(s, j, p)
        ktb[s, :, :LOOK * block] = jnp.transpose(kvb[s, :LOOK * block, :size])
        for k in range(chunks):
            compute(s, h, k, k == 0, False, range(LOOK), started[s, k])

    for i, t in enumerate(others):
        pltpu.make_async_copy(aux_r.at[t], aux_r.at[t], aux_recv_sem.at[t]).wait()
    for s in range(2):
        for k in range(chunks):
            for i, t in enumerate(others):
                for a, buf in enumerate((qb, gb)):
                    part = buf.at[s, t, :, pl.ds(k * chunk_heads * size, chunk_heads * size)]
                    pltpu.make_async_copy(part, part, y_recv.at[s, k, t, a]).wait()
                compute(s, t, k, False, k == chunks - 1 and i == n_kvh - 2, range(LOOK + 1))

    for s in range(2):
        own = slice(LOOK * block, (LOOK + 1) * block)
        b = ids[s]
        dk_acc[s, own, :] = dk_acc[s, own, :] * scale
        for slot, valid in ((1, even[s] | (b + 3 < n_blocks)), (0, b + 2 < n_blocks)):
            @pl.when(valid)
            def _():
                pltpu.make_async_copy(rb.at[s, slot], rb.at[s, slot], d_recv.at[s, slot]).wait()
                dk_acc[s, own, :] += rb[s, slot, :, :size].astype(F32)
                dv_acc[s, own, :] += rb[s, slot, :, size:].astype(F32)

        dk_ref[s] = dk_acc[s, own, :].astype(BF16)
        dv_ref[s] = dv_acc[s, own, :].astype(BF16)

    for cp in kvy + ysent + auxsent:
        cp.wait_send()
    for valid, cp in sent:
        pl.when(valid)(cp.wait_send)


def write_out(*refs):
    copies = [
        pltpu.make_async_copy(refs[i], refs[3 + i], refs[6].at[i]) for i in range(3)
    ]
    for cp in copies:
        cp.start()
    for cp in copies:
        cp.wait()


def body(
    doc_lengths,
    queries,
    key_matrix,
    value_matrix,
    forward_output,
    output_cotangent,
    log_normalizer_rows,
):
    n_ctx, n_kvh = lax.axis_size("ctx"), lax.axis_size("kvh")
    rows = queries.shape[1]
    group = queries.shape[2] // key_matrix.shape[2]
    size = key_matrix.shape[2] // n_kvh
    block = rows * n_kvh
    width = group * size
    chunk_heads = max(1, min(group, 256 // rows))
    chunks = group // chunk_heads
    dims = (n_ctx, n_kvh, rows, group, size, chunk_heads, doc_lengths.shape[0])
    peers = n_kvh - 1
    lanes = chunk_heads * rows
    aux_rows = -(-4 * chunks // 8) * 8
    dma = pltpu.SemaphoreType.DMA
    anywhere = pl.BlockSpec(memory_space=pl.ANY)
    vmem = pl.BlockSpec(memory_space=pltpu.VMEM)
    grads = pl.pallas_call(
        functools.partial(kernel, dims),
        out_shape=(
            pltpu.VMEM((2, block, width), BF16),
            pltpu.VMEM((2, block, size), BF16),
            pltpu.VMEM((2, block, size), BF16),
        ),
        in_specs=[anywhere] * 7,
        out_specs=(vmem, vmem, vmem),
        scratch_shapes=[
            pltpu.SMEM(doc_lengths.shape, jnp.int32),
            pltpu.VMEM((2, group * n_kvh, rows), F32),
            pltpu.VMEM((2, n_kvh, rows, width), BF16),
            pltpu.VMEM((2, n_kvh, rows, width), BF16),
            pltpu.VMEM((2, rows, width * n_kvh), BF16),
            pltpu.VMEM((2, rows, width * n_kvh), BF16),
            pltpu.VMEM((2, (LOOK + 1) * block, 2 * size), BF16),
            pltpu.VMEM((2, size, (LOOK + 1) * block), BF16),
            pltpu.VMEM((2, (LOOK + 1) * block, size), F32),
            pltpu.VMEM((2, (LOOK + 1) * block, size), F32),
            pltpu.VMEM((2, 3, block, 2 * size), BF16),
            pltpu.VMEM((2, 3, block, 2 * size), BF16),
            pltpu.VMEM((n_kvh, aux_rows, lanes), F32),
            pltpu.VMEM((n_kvh, aux_rows, lanes), F32),
            dma((6,)),
            dma((2, 2)),
            dma((2, chunks, peers, 2)),
            dma((2, chunks, n_kvh, 2)),
            dma((2, peers, 2)),
            dma((2, n_kvh)),
            dma((2, 3, n_kvh)),
            dma((2, LOOK, n_kvh)),
            dma((peers,)),
            dma((n_kvh,)),
            dma((2, 3)),
            dma((2, 3)),
            pltpu.SemaphoreType.REGULAR((2,)),
        ],
        compiler_params=pltpu.CompilerParams(collective_id=0, has_side_effects=True),
    )(
        doc_lengths, jnp.transpose(log_normalizer_rows, (0, 2, 1)), queries, key_matrix, value_matrix,
        forward_output, output_cotangent,
    )
    return pl.pallas_call(
        write_out,
        out_shape=tuple(jax.ShapeDtypeStruct(x.shape, x.dtype) for x in grads),
        in_specs=[vmem] * 3,
        out_specs=[anywhere] * 3,
        scratch_shapes=[dma((3,))],
    )(*[pltpu.with_memory_space_constraint(x, pltpu.VMEM) for x in grads])


def solution(mesh):
    rows = P(None, ("ctx", "kvh"), None)
    return jax.shard_map(
        body,
        mesh=mesh,
        in_specs=(P(),) + (rows,) * 6,
        out_specs=(P(None, "ctx", "kvh"),) * 3,
        check_vma=False,
    )
```

```python
import functools

import jax
import jax.numpy as jnp
from jax import lax
from jax.experimental import pallas as pl
from jax.experimental.pallas import tpu as pltpu
from jax.sharding import PartitionSpec as P

LOOK = 3
MESH = pl.DeviceIdType.MESH
F32 = jnp.float32
BF16 = jnp.bfloat16
NT = (((1,), (1,)), ((), ()))


def row_sums(values, terms):
    ones = jnp.ones((8, values.shape[1]), BF16)
    total, rest = None, values
    for _ in range(terms):
        part = rest.astype(BF16)
        rest = rest - part.astype(F32)
        term = lax.dot_general(ones, part, NT, preferred_element_type=F32)
        total = term if total is None else total + term
    return total


def kernel(
    dims,
    docs_hbm, lse_hbm, q_hbm, k_hbm, v_hbm, o_hbm, g_hbm,
    dqo, dk_ref, dv_ref,
    docs_ref, lse_ref, qb, gb, gl, ol, kvb, ktb, dk_acc, dv_acc, sb, rb, aux_s, aux_r,
    loc_sem, kvl_sem, y_send, y_recv, kvy_send, kvy_recv, kv_send, kv_recv,
    aux_send_sem, aux_recv_sem, d_send, d_recv, gate,
):
    n_ctx, n_kvh, rows, group, size, chunk_heads, n_docs = dims
    block = n_kvh * rows
    width = group * size
    chunks = group // chunk_heads
    lanes = chunk_heads * rows
    n_blocks = 2 * n_ctx
    scale = size ** -0.5
    c = lax.axis_index("ctx")
    h = lax.axis_index("kvh")
    ids = (c, n_blocks - 1 - c)
    odd = lax.rem(c, 2)
    pair = c + 1 - 2 * odd
    even = (odd == 0, odd == 1)
    others = [lax.rem(h + i, n_kvh) for i in range(1, n_kvh)]

    def place(b):
        return jnp.where(b < n_ctx, b, n_blocks - 1 - b), jnp.where(b < n_ctx, 0, 1)

    def mult(x, m):
        return pl.multiple_of(x, m)

    def tile(j, p=None):
        if p is None:
            return pl.ds(mult(j * block, block), block)
        return pl.ds(mult(j * block + p * rows, rows), rows)

    barrier = pltpu.get_barrier_semaphore()
    leader = n_kvh - 1

    def signal(sem, **device):
        pl.semaphore_signal(sem, inc=1, device_id=device, device_id_type=MESH)

    @pl.when(h != leader)
    def _():
        signal(barrier, kvh=leader)

    @pl.when(h == leader)
    def _():
        if leader:
            pl.semaphore_wait(barrier, leader)
        for t in range(leader):
            signal(gate.at[0], kvh=t)

    own_cols = pl.ds(mult(h * width, width), width)
    own_key = pl.ds(mult(h * size, size), size)
    kv_local = []
    for s in range(2):
        for a, src in enumerate((k_hbm, v_hbm)):
            cp = pltpu.make_async_copy(
                src.at[s, :, own_key],
                kvb.at[s, tile(LOOK, h), pl.ds(a * size, size)],
                kvl_sem.at[s, a],
            )
            kv_local.append(cp)
    local = [
        pltpu.make_async_copy(g_hbm, gl, loc_sem.at[0]),
        pltpu.make_async_copy(o_hbm, ol, loc_sem.at[1]),
        pltpu.make_async_copy(q_hbm.at[:, :, own_cols], qb.at[:, h], loc_sem.at[2]),
        pltpu.make_async_copy(g_hbm.at[:, :, own_cols], gb.at[:, h], loc_sem.at[3]),
        pltpu.make_async_copy(lse_hbm, lse_ref, loc_sem.at[4]),
        pltpu.make_async_copy(docs_hbm, docs_ref, loc_sem.at[5]),
    ]

    def start_local():
        for cp in local[:2] + local[4:] + kv_local + local[2:4]:
            cp.start()

    @pl.when(h != leader)
    def _():
        start_local()
        pl.semaphore_wait(gate.at[0], 1)

    kvy, ysent, auxsent, sent = [], [], [], []
    for s in range(2):
        for i, t in enumerate(others):
            for a, src in enumerate((k_hbm, v_hbm)):
                cp = pltpu.make_async_remote_copy(
                    src.at[s, :, pl.ds(mult(t * size, size), size)],
                    kvb.at[s, tile(LOOK, h), pl.ds(a * size, size)],
                    kvy_send.at[s, i, a],
                    kvy_recv.at[s, h],
                    device_id={"kvh": t},
                    device_id_type=MESH,
                )
                cp.start()
                kvy.append(cp)

    def send_chunk(s, k):
        for i, t in enumerate(others):
            for a, (src, dst) in enumerate(((q_hbm, qb), (g_hbm, gb))):
                span = chunk_heads * size
                cp = pltpu.make_async_remote_copy(
                    src.at[s, :, pl.ds(mult(t * width + k * span, span), span)],
                    dst.at[s, h, :, pl.ds(k * span, span)],
                    y_send.at[s, k, i, a],
                    y_recv.at[s, k, h, a],
                    device_id={"kvh": t},
                    device_id_type=MESH,
                )
                cp.start()
                ysent.append(cp)

    send_chunk(0, 0)
    pl.when(h == leader)(start_local)
    near = [(ctx, (ctx >= 0) & (ctx < n_ctx)) for ctx in (c - 2, c + 2, c - 3 + 6 * odd)]

    @pl.when(h == 0)
    def _():
        signal(barrier, ctx=pair)
        for ctx, inside in near:
            @pl.when(inside)
            def _():
                signal(barrier, ctx=ctx)

    for s in range(2):
        for d in range(1, LOOK + 1):
            @pl.when(ids[s] - d < 0)
            def _():
                kvb[s, (LOOK - d) * block:(LOOK - d + 1) * block, :] = jnp.zeros(
                    (block, 2 * size), BF16
                )
    def send(valid, src, dst, send_sem, recv_sem, ctx):
        cp = pltpu.make_async_remote_copy(
            src, dst, send_sem, recv_sem, device_id={"ctx": ctx}, device_id_type=MESH
        )
        pl.when(valid)(cp.start)
        sent.append((valid, cp))

    def spread(s):
        b, src = ids[s], kvb.at[s, tile(LOOK), :]
        ctx, half = place(b + 2)
        send(
            b + 2 < n_blocks, src, kvb.at[half, tile(1), :],
            kv_send.at[s, 0], kv_recv.at[half, 1], ctx,
        )
        ctx, half = place(b + 3)
        j = jnp.where(even[s], 2, 0)
        ctx, half = jnp.where(even[s], pair, ctx), jnp.where(even[s], s, half)
        send(
            even[s] | (b + 3 < n_blocks), src, kvb.at[half, tile(j), :],
            kv_send.at[s, 1], kv_recv.at[half, j], ctx,
        )

    def wait_tile(s, j):
        part = kvb.at[s, tile(j), :]
        pl.when(ids[s] - (LOOK - j) >= 0)(
            pltpu.make_async_copy(part, part, kv_recv.at[s, j]).wait
        )

    def forward(s):
        wait_tile(s, 1)
        j = jnp.where(even[s], 0, 2)
        send(
            ids[s] >= 2, kvb.at[s, tile(1), :], kvb.at[s, tile(j), :],
            kv_send.at[s, 2], kv_recv.at[s, j], pair,
        )

    local[0].wait()
    local[1].wait()
    local[4].wait()

    def fill_aux(g):
        cols = pl.ds(mult(g * width, width), width)
        for s in range(2):
            prods = gl[s, :, cols].astype(F32) * ol[s, :, cols].astype(F32)
            delta = row_sums(
                jnp.concatenate([prods[:, i * size:(i + 1) * size] for i in range(group)], axis=0), 2
            )
            for k in range(chunks):
                r = 2 * (s * chunks + k)
                aux_s[g, r + 1:r + 2, :] = delta[:1, k * lanes:(k + 1) * lanes]
                lse = lse_ref[s, pl.ds(mult(g * group + k * chunk_heads, chunk_heads), chunk_heads), :]
                for i in range(chunk_heads):
                    aux_s[g, r:r + 1, i * rows:(i + 1) * rows] = lse[i:i + 1]

    for i, t in enumerate(others):
        fill_aux(t)
        cp = pltpu.make_async_remote_copy(
            aux_s.at[t], aux_r.at[h], aux_send_sem.at[i], aux_recv_sem.at[h],
            device_id={"kvh": t}, device_id_type=MESH,
        )
        cp.start()
        auxsent.append(cp)
    for s in range(2):
        for k in range(chunks):
            if s + k:
                send_chunk(s, k)
    @pl.when(h == 0)
    def _():
        count = jnp.int32(1)
        for _, inside in near:
            count = count + inside.astype(jnp.int32)
        pl.semaphore_wait(barrier, count)
        for t in range(1, n_kvh):
            signal(gate.at[1], kvh=t)

    @pl.when(h != 0)
    def _():
        pl.semaphore_wait(gate.at[1], 1)

    for cp in kv_local:
        cp.wait()
    for s in range(2):
        for t in others:
            part = kvb.at[s, tile(LOOK, t), :]
            pltpu.make_async_copy(part, part, kvy_recv.at[s, t]).wait()
        spread(s)
    fill_aux(h)
    aux_r[h] = aux_s[h]

    own_span = slice(LOOK * block, (LOOK + 1) * block)
    local[5].wait()
    ends, total = [], jnp.int32(0)
    for i in range(n_docs):
        total = total + docs_ref[i]
        ends.append(total)
    spot = lax.broadcasted_iota(jnp.int32, (1, lanes), 1) % rows
    key_spot = lax.broadcasted_iota(jnp.int32, (block, lanes), 0)

    def stage(s, slot, dk, dv):
        sb[s, slot, :, :size] = (dk * scale).astype(BF16)
        sb[s, slot, :, size:] = dv.astype(BF16)

    def send_exchange(s, j):
        stage(s, 0, dk_acc[s, tile(j), :], dv_acc[s, tile(j), :])
        send(ids[s] >= 2, sb.at[s, 0], rb.at[s, 2], d_send.at[s, 0], d_recv.at[s, 2], pair)

    def send_direct(s, j):
        stage(s, 1, dk_acc[s, tile(j), :], dv_acc[s, tile(j), :])
        b = ids[s]
        ctx, half = place(b - 3)
        ctx, half = jnp.where(even[s], ctx, pair), jnp.where(even[s], half, s)
        send(
            (~even[s]) | (b - 3 >= 0), sb.at[s, 1], rb.at[half, 1],
            d_send.at[s, 1], d_recv.at[half, 1], ctx,
        )

    def send_combined(s):
        b = ids[s]
        ctx, half = place(b - 2)

        @pl.when(b >= 2)
        def _():
            pltpu.make_async_copy(rb.at[s, 2], rb.at[s, 2], d_recv.at[s, 2]).wait()
            sb[s, 2, :, :size] = (
                dk_acc[s, block:2 * block, :] * scale + rb[s, 2, :, :size].astype(F32)
            ).astype(BF16)
            sb[s, 2, :, size:] = (
                dv_acc[s, block:2 * block, :] + rb[s, 2, :, size:].astype(F32)
            ).astype(BF16)

        send(b >= 2, sb.at[s, 2], rb.at[half, 0], d_send.at[s, 2], d_recv.at[half, 0], ctx)

    def compute(s, p, k, first, last, tiles, dqt=None, finish=True, arrival=None):
        heads = range(k * chunk_heads, (k + 1) * chunk_heads)
        if arrival:
            arrival[0].wait()
        q = jnp.concatenate([qb[s, p, :, n * size:(n + 1) * size] for n in heads], axis=0)
        r = 2 * (s * chunks + k)
        norm = aux_r[p, r:r + 1, :]
        delta = aux_r[p, r + 1:r + 2, :]
        pos = ids[s] * block + p * rows + spot
        start = jnp.zeros_like(pos)
        for end in ends:
            start = jnp.where(pos >= end, end, start)
        base = (ids[s] - LOOK) * block
        pos, start = pos - base, start - base
        if last:
            tiles = [jnp.where(even[s], 2, 0), jnp.where(even[s], 0, 2), 1, LOOK]
        lo, hi = (tiles[0], tiles[-1]) if not last else (0, LOOK)
        span = slice(lo * block, (hi + 1) * block)
        size_k = (hi + 1 - lo) * block
        st = lax.dot_general(kvb[s, span, :size], q, NT, preferred_element_type=F32)
        t = lax.broadcasted_iota(jnp.int32, (size_k, lanes), 0) + lo * block
        allowed = t >= start
        if hi == LOOK:
            allowed = allowed & (t <= pos)
        w = jnp.where(allowed, jnp.exp(st * scale - norm), 0.0)
        if arrival:
            arrival[1].wait()
        g = jnp.concatenate([gb[s, p, :, n * size:(n + 1) * size] for n in heads], axis=0)
        dv = jnp.dot(w.astype(BF16), g, preferred_element_type=F32)
        dp = lax.dot_general(kvb[s, span, size:], g, NT, preferred_element_type=F32)
        ds = (w * (dp - delta)).astype(BF16)
        dk = jnp.dot(ds, q, preferred_element_type=F32)
        if first:
            dv_acc[s, span, :] = dv
            dk_acc[s, span, :] = dk
        else:
            dv_acc[s, span, :] += dv
            dk_acc[s, span, :] += dk
        part = jnp.dot(ktb[s, :, span], ds, preferred_element_type=F32)
        dqt = part if dqt is None else dqt + part
        if last:
            send_exchange(s, jnp.where(even[s], 2, 0))
            send_direct(s, jnp.where(even[s], 0, 2))
        if last and s:
            send_combined(s)
        if not finish:
            return dqt
        dq = (jnp.transpose(dqt) * scale).astype(BF16)
        for i, n in enumerate(heads):
            dqo[s, pl.ds(mult(p * rows, rows), rows), n * size:(n + 1) * size] = dq[i * rows:(i + 1) * rows]

    local[2].wait()
    local[3].wait()
    def arrival(s, k, t):
        copies = []
        for a, buf in enumerate((qb, gb)):
            part = buf.at[s, t, :, pl.ds(k * chunk_heads * size, chunk_heads * size)]
            copies.append(pltpu.make_async_copy(part, part, y_recv.at[s, k, t, a]))
        return copies

    started = {}
    for s in range(2):
        ktb[s, :, own_span] = jnp.transpose(kvb[s, own_span, :size])
        for k in range(chunks):
            started[s, k, -1] = compute(s, h, k, k == 0, False, [LOOK], None, False)
        forward(s)
    for i, t in enumerate(others):
        pltpu.make_async_copy(aux_r.at[t], aux_r.at[t], aux_recv_sem.at[t]).wait()
        if chunks > 1:
            started[0, 0, i] = compute(0, t, 0, False, False, [LOOK], None, False, arrival(0, 0, t))
    for s in range(2):
        wait_tile(s, 0)
        wait_tile(s, 2)
        ktb[s, :, :LOOK * block] = jnp.transpose(kvb[s, :LOOK * block, :size])
        for k in range(chunks):
            compute(s, h, k, k == 0, False, range(LOOK), started[s, k, -1])
        if s:
            send_combined(0)
        for k in range(chunks):
            for i, t in enumerate(others):
                last = k == chunks - 1 and i == n_kvh - 2
                if (s, k, i) in started:
                    compute(s, t, k, False, last, range(LOOK), started[s, k, i])
                else:
                    compute(s, t, k, False, last, range(LOOK + 1), arrival=arrival(s, k, t))
    early_sends = len(sent) - 3
    for cp in kvy + ysent + auxsent:
        cp.wait_send()
    for valid, cp in sent[:early_sends]:
        pl.when(valid)(cp.wait_send)
    for s in range(2):
        own = slice(LOOK * block, (LOOK + 1) * block)
        b = ids[s]
        dk_acc[s, own, :] = dk_acc[s, own, :] * scale
        for slot, valid in ((1, even[s] | (b + 3 < n_blocks)), (0, b + 2 < n_blocks)):
            @pl.when(valid)
            def _():
                pltpu.make_async_copy(rb.at[s, slot], rb.at[s, slot], d_recv.at[s, slot]).wait()
                dk_acc[s, own, :] += rb[s, slot, :, :size].astype(F32)
                dv_acc[s, own, :] += rb[s, slot, :, size:].astype(F32)

        dk_ref[s] = dk_acc[s, own, :].astype(BF16)
        dv_ref[s] = dv_acc[s, own, :].astype(BF16)

    for valid, cp in sent[early_sends:]:
        pl.when(valid)(cp.wait_send)


def write_out(*refs):
    copies = [
        pltpu.make_async_copy(refs[i], refs[3 + i], refs[6].at[i]) for i in range(3)
    ]
    for cp in copies:
        cp.start()
    for cp in copies:
        cp.wait()


def body(
    doc_lengths,
    queries,
    key_matrix,
    value_matrix,
    forward_output,
    output_cotangent,
    log_normalizer_rows,
):
    n_ctx, n_kvh = lax.axis_size("ctx"), lax.axis_size("kvh")
    rows = queries.shape[1]
    group = queries.shape[2] // key_matrix.shape[2]
    size = key_matrix.shape[2] // n_kvh
    block = rows * n_kvh
    width = group * size
    chunk_heads = max(1, min(group, 256 // rows))
    chunks = group // chunk_heads
    dims = (n_ctx, n_kvh, rows, group, size, chunk_heads, doc_lengths.shape[0])
    peers = n_kvh - 1
    lanes = chunk_heads * rows
    aux_rows = -(-4 * chunks // 8) * 8
    dma = pltpu.SemaphoreType.DMA
    anywhere = pl.BlockSpec(memory_space=pl.ANY)
    vmem = pl.BlockSpec(memory_space=pltpu.VMEM)
    grads = pl.pallas_call(
        functools.partial(kernel, dims),
        out_shape=(
            pltpu.VMEM((2, block, width), BF16),
            pltpu.VMEM((2, block, size), BF16),
            pltpu.VMEM((2, block, size), BF16),
        ),
        in_specs=[anywhere] * 7,
        out_specs=(vmem, vmem, vmem),
        scratch_shapes=[
            pltpu.SMEM(doc_lengths.shape, jnp.int32),
            pltpu.VMEM((2, group * n_kvh, rows), F32),
            pltpu.VMEM((2, n_kvh, rows, width), BF16),
            pltpu.VMEM((2, n_kvh, rows, width), BF16),
            pltpu.VMEM((2, rows, width * n_kvh), BF16),
            pltpu.VMEM((2, rows, width * n_kvh), BF16),
            pltpu.VMEM((2, (LOOK + 1) * block, 2 * size), BF16),
            pltpu.VMEM((2, size, (LOOK + 1) * block), BF16),
            pltpu.VMEM((2, (LOOK + 1) * block, size), F32),
            pltpu.VMEM((2, (LOOK + 1) * block, size), F32),
            pltpu.VMEM((2, 3, block, 2 * size), BF16),
            pltpu.VMEM((2, 3, block, 2 * size), BF16),
            pltpu.VMEM((n_kvh, aux_rows, lanes), F32),
            pltpu.VMEM((n_kvh, aux_rows, lanes), F32),
            dma((6,)),
            dma((2, 2)),
            dma((2, chunks, peers, 2)),
            dma((2, chunks, n_kvh, 2)),
            dma((2, peers, 2)),
            dma((2, n_kvh)),
            dma((2, 3)),
            dma((2, LOOK)),
            dma((peers,)),
            dma((n_kvh,)),
            dma((2, 3)),
            dma((2, 3)),
            pltpu.SemaphoreType.REGULAR((2,)),
        ],
        compiler_params=pltpu.CompilerParams(collective_id=0, has_side_effects=True),
    )(
        doc_lengths, jnp.transpose(log_normalizer_rows, (0, 2, 1)), queries, key_matrix, value_matrix,
        forward_output, output_cotangent,
    )
    return pl.pallas_call(
        write_out,
        out_shape=tuple(jax.ShapeDtypeStruct(x.shape, x.dtype) for x in grads),
        in_specs=[vmem] * 3,
        out_specs=[anywhere] * 3,
        scratch_shapes=[dma((3,))],
    )(*[pltpu.with_memory_space_constraint(x, pltpu.VMEM) for x in grads])


def solution(mesh):
    rows = P(None, ("ctx", "kvh"), None)
    return jax.shard_map(
        body,
        mesh=mesh,
        in_specs=(P(),) + (rows,) * 6,
        out_specs=(P(None, "ctx", "kvh"),) * 3,
        check_vma=False,
    )
```

```python
import functools

import jax
import jax.numpy as jnp
from jax import lax
from jax.experimental import pallas as pl
from jax.experimental.pallas import tpu as pltpu
from jax.sharding import PartitionSpec as P

LOOK = 3
MESH = pl.DeviceIdType.MESH
F32 = jnp.float32
BF16 = jnp.bfloat16
NT = (((1,), (1,)), ((), ()))


def row_sums(values, terms):
    ones = jnp.ones((8, values.shape[1]), BF16)
    total, rest = None, values
    for _ in range(terms):
        part = rest.astype(BF16)
        rest = rest - part.astype(F32)
        term = lax.dot_general(ones, part, NT, preferred_element_type=F32)
        total = term if total is None else total + term
    return total


def kernel(
    dims,
    docs_hbm, lse_hbm, q_hbm, k_hbm, v_hbm, o_hbm, g_hbm,
    dqo, dk_ref, dv_ref,
    docs_ref, lse_ref, qb, gb, gl, ol, kvb, ktb, dk_acc, dv_acc, sb, rb, aux_s, aux_r,
    loc_sem, kvl_sem, y_send, y_recv, kvy_send, kvy_recv, kv_send, kv_recv,
    aux_send_sem, aux_recv_sem, d_send, d_recv, gate,
):
    n_ctx, n_kvh, rows, group, size, chunk_heads, n_docs = dims
    block = n_kvh * rows
    width = group * size
    chunks = group // chunk_heads
    lanes = chunk_heads * rows
    n_blocks = 2 * n_ctx
    scale = size ** -0.5
    c = lax.axis_index("ctx")
    h = lax.axis_index("kvh")
    ids = (c, n_blocks - 1 - c)
    odd = lax.rem(c, 2)
    pair = c + 1 - 2 * odd
    even = (odd == 0, odd == 1)
    others = [lax.rem(h + i, n_kvh) for i in range(1, n_kvh)]

    def place(b):
        return jnp.where(b < n_ctx, b, n_blocks - 1 - b), jnp.where(b < n_ctx, 0, 1)

    def mult(x, m):
        return pl.multiple_of(x, m)

    def tile(j, p=None):
        if p is None:
            return pl.ds(mult(j * block, block), block)
        return pl.ds(mult(j * block + p * rows, rows), rows)

    barrier = pltpu.get_barrier_semaphore()
    leader = n_kvh - 1

    def signal(sem, **device):
        pl.semaphore_signal(sem, inc=1, device_id=device, device_id_type=MESH)

    @pl.when(h != leader)
    def _():
        signal(barrier, kvh=leader)

    @pl.when(h == leader)
    def _():
        if leader:
            pl.semaphore_wait(barrier, leader)
        for t in range(leader):
            signal(gate.at[0], kvh=t)

    own_cols = pl.ds(mult(h * width, width), width)
    own_key = pl.ds(mult(h * size, size), size)
    kv_local = []
    for s in range(2):
        for a, src in enumerate((k_hbm, v_hbm)):
            cp = pltpu.make_async_copy(
                src.at[s, :, own_key],
                kvb.at[s, tile(LOOK, h), pl.ds(a * size, size)],
                kvl_sem.at[s, a],
            )
            kv_local.append(cp)
    local = [
        pltpu.make_async_copy(g_hbm, gl, loc_sem.at[0]),
        pltpu.make_async_copy(o_hbm, ol, loc_sem.at[1]),
        pltpu.make_async_copy(q_hbm.at[:, :, own_cols], qb.at[:, h], loc_sem.at[2]),
        pltpu.make_async_copy(g_hbm.at[:, :, own_cols], gb.at[:, h], loc_sem.at[3]),
        pltpu.make_async_copy(lse_hbm, lse_ref, loc_sem.at[4]),
        pltpu.make_async_copy(docs_hbm, docs_ref, loc_sem.at[5]),
    ]

    def start_local():
        for cp in local[:2] + local[4:] + kv_local + local[2:4]:
            cp.start()

    @pl.when(h != leader)
    def _():
        start_local()
        pl.semaphore_wait(gate.at[0], 1)

    kvy, ysent, auxsent, sent = [], [], [], []
    for s in range(2):
        for i, t in enumerate(others):
            for a, src in enumerate((k_hbm, v_hbm)):
                cp = pltpu.make_async_remote_copy(
                    src.at[s, :, pl.ds(mult(t * size, size), size)],
                    kvb.at[s, tile(LOOK, h), pl.ds(a * size, size)],
                    kvy_send.at[s, i, a],
                    kvy_recv.at[s, h],
                    device_id={"kvh": t},
                    device_id_type=MESH,
                )
                cp.start()
                kvy.append(cp)

    def send_chunk(s, k):
        for i, t in enumerate(others):
            for a, (src, dst) in enumerate(((q_hbm, qb), (g_hbm, gb))):
                span = chunk_heads * size
                cp = pltpu.make_async_remote_copy(
                    src.at[s, :, pl.ds(mult(t * width + k * span, span), span)],
                    dst.at[s, h, :, pl.ds(k * span, span)],
                    y_send.at[s, k, i, a],
                    y_recv.at[s, k, h, a],
                    device_id={"kvh": t},
                    device_id_type=MESH,
                )
                cp.start()
                ysent.append(cp)

    send_chunk(0, 0)
    pl.when(h == leader)(start_local)
    near = [(ctx, (ctx >= 0) & (ctx < n_ctx)) for ctx in (c - 2, c + 2, c - 3 + 6 * odd)]

    @pl.when(h == 0)
    def _():
        signal(barrier, ctx=pair)
        for ctx, inside in near:
            @pl.when(inside)
            def _():
                signal(barrier, ctx=ctx)

    for s in range(2):
        for d in range(1, LOOK + 1):
            @pl.when(ids[s] - d < 0)
            def _():
                kvb[s, (LOOK - d) * block:(LOOK - d + 1) * block, :] = jnp.zeros(
                    (block, 2 * size), BF16
                )
    def send(valid, src, dst, send_sem, recv_sem, ctx):
        cp = pltpu.make_async_remote_copy(
            src, dst, send_sem, recv_sem, device_id={"ctx": ctx}, device_id_type=MESH
        )
        pl.when(valid)(cp.start)
        sent.append((valid, cp))

    def spread(s):
        b, src = ids[s], kvb.at[s, tile(LOOK), :]
        ctx, half = place(b + 2)
        send(
            b + 2 < n_blocks, src, kvb.at[half, tile(1), :],
            kv_send.at[s, 0], kv_recv.at[half, 1], ctx,
        )
        ctx, half = place(b + 3)
        j = jnp.where(even[s], 2, 0)
        ctx, half = jnp.where(even[s], pair, ctx), jnp.where(even[s], s, half)
        send(
            even[s] | (b + 3 < n_blocks), src, kvb.at[half, tile(j), :],
            kv_send.at[s, 1], kv_recv.at[half, j], ctx,
        )

    def wait_tile(s, j):
        part = kvb.at[s, tile(j), :]
        pl.when(ids[s] - (LOOK - j) >= 0)(
            pltpu.make_async_copy(part, part, kv_recv.at[s, j]).wait
        )

    def forward(s):
        wait_tile(s, 1)
        j = jnp.where(even[s], 0, 2)
        send(
            ids[s] >= 2, kvb.at[s, tile(1), :], kvb.at[s, tile(j), :],
            kv_send.at[s, 2], kv_recv.at[s, j], pair,
        )

    local[0].wait()
    local[1].wait()
    local[4].wait()

    def fill_aux(g):
        cols = pl.ds(mult(g * width, width), width)
        for s in range(2):
            prods = gl[s, :, cols].astype(F32) * ol[s, :, cols].astype(F32)
            delta = row_sums(
                jnp.concatenate([prods[:, i * size:(i + 1) * size] for i in range(group)], axis=0), 2
            )
            for k in range(chunks):
                r = 2 * (s * chunks + k)
                aux_s[g, r + 1:r + 2, :] = delta[:1, k * lanes:(k + 1) * lanes]
                lse = lse_ref[s, pl.ds(mult(g * group + k * chunk_heads, chunk_heads), chunk_heads), :]
                for i in range(chunk_heads):
                    aux_s[g, r:r + 1, i * rows:(i + 1) * rows] = lse[i:i + 1]

    for i, t in enumerate(others):
        fill_aux(t)
        cp = pltpu.make_async_remote_copy(
            aux_s.at[t], aux_r.at[h], aux_send_sem.at[i], aux_recv_sem.at[h],
            device_id={"kvh": t}, device_id_type=MESH,
        )
        cp.start()
        auxsent.append(cp)
    for s in range(2):
        for k in range(chunks):
            if s + k:
                send_chunk(s, k)
    @pl.when(h == 0)
    def _():
        count = jnp.int32(1)
        for _, inside in near:
            count = count + inside.astype(jnp.int32)
        pl.semaphore_wait(barrier, count)
        for t in range(1, n_kvh):
            signal(gate.at[1], kvh=t)

    @pl.when(h != 0)
    def _():
        pl.semaphore_wait(gate.at[1], 1)

    for cp in kv_local:
        cp.wait()
    for s in range(2):
        for t in others:
            part = kvb.at[s, tile(LOOK, t), :]
            pltpu.make_async_copy(part, part, kvy_recv.at[s, t]).wait()
        spread(s)
    fill_aux(h)
    aux_r[h] = aux_s[h]

    own_span = slice(LOOK * block, (LOOK + 1) * block)
    local[5].wait()
    ends, total = [], jnp.int32(0)
    for i in range(n_docs):
        total = total + docs_ref[i]
        ends.append(total)
    spot = lax.broadcasted_iota(jnp.int32, (1, lanes), 1) % rows
    key_spot = lax.broadcasted_iota(jnp.int32, (block, lanes), 0)

    def stage(s, slot, dk, dv):
        sb[s, slot, :, :size] = (dk * scale).astype(BF16)
        sb[s, slot, :, size:] = dv.astype(BF16)

    def send_exchange(s, j):
        stage(s, 0, dk_acc[s, tile(j), :], dv_acc[s, tile(j), :])
        ctx, half, slot = pair, s, 2
        if s == 1:
            ctx, half = place(ids[s] - 3)
            ctx, half = jnp.where(even[s], pair, ctx), jnp.where(even[s], s, half)
            slot = jnp.where(even[s], 2, 3)
        here = ctx == c
        send(
            (ids[s] >= 2) & ~here, sb.at[s, 0], rb.at[half, slot],
            d_send.at[s, 0], d_recv.at[half, slot], ctx,
        )
        if s == 1:
            stay = pltpu.make_async_copy(sb.at[s, 0], rb.at[half, slot], d_recv.at[half, slot])
            pl.when(here)(stay.start)

    def send_direct(s, j):
        stage(s, 1, dk_acc[s, tile(j), :], dv_acc[s, tile(j), :])
        b = ids[s]
        ctx, half = place(b - 3)
        ctx, half = jnp.where(even[s], ctx, pair), jnp.where(even[s], half, s)
        send(
            (~even[s]) | (b - 3 >= 0), sb.at[s, 1], rb.at[half, 1],
            d_send.at[s, 1], d_recv.at[half, 1], ctx,
        )

    def send_combined(s):
        b = ids[s]
        ctx, half = place(b - 2)

        if s == 1:
            @pl.when(even[s])
            def _():
                stage(s, 2, dk_acc[s, block:2 * block, :], dv_acc[s, block:2 * block, :])

        @pl.when((b >= 2) & ~even[s] if s == 1 else b >= 2)
        def _():
            pltpu.make_async_copy(rb.at[s, 2], rb.at[s, 2], d_recv.at[s, 2]).wait()
            sb[s, 2, :, :size] = (
                dk_acc[s, block:2 * block, :] * scale + rb[s, 2, :, :size].astype(F32)
            ).astype(BF16)
            sb[s, 2, :, size:] = (
                dv_acc[s, block:2 * block, :] + rb[s, 2, :, size:].astype(F32)
            ).astype(BF16)

        send(b >= 2, sb.at[s, 2], rb.at[half, 0], d_send.at[s, 2], d_recv.at[half, 0], ctx)

    def compute(s, p, k, first, last, tiles, dqt=None, finish=True, arrival=None):
        heads = range(k * chunk_heads, (k + 1) * chunk_heads)
        if arrival:
            arrival[0].wait()
        q = jnp.concatenate([qb[s, p, :, n * size:(n + 1) * size] for n in heads], axis=0)
        r = 2 * (s * chunks + k)
        norm = aux_r[p, r:r + 1, :]
        delta = aux_r[p, r + 1:r + 2, :]
        pos = ids[s] * block + p * rows + spot
        start = jnp.zeros_like(pos)
        for end in ends:
            start = jnp.where(pos >= end, end, start)
        base = (ids[s] - LOOK) * block
        pos, start = pos - base, start - base
        if last:
            tiles = [jnp.where(even[s], 2, 0), jnp.where(even[s], 0, 2), 1, LOOK]
        lo, hi = (tiles[0], tiles[-1]) if not last else (0, LOOK)
        span = slice(lo * block, (hi + 1) * block)
        size_k = (hi + 1 - lo) * block
        st = lax.dot_general(kvb[s, span, :size], q, NT, preferred_element_type=F32)
        t = lax.broadcasted_iota(jnp.int32, (size_k, lanes), 0) + lo * block
        allowed = t >= start
        if hi == LOOK:
            allowed = allowed & (t <= pos)
        w = jnp.where(allowed, jnp.exp(st * scale - norm), 0.0)
        if arrival:
            arrival[1].wait()
        g = jnp.concatenate([gb[s, p, :, n * size:(n + 1) * size] for n in heads], axis=0)
        dv = jnp.dot(w.astype(BF16), g, preferred_element_type=F32)
        dp = lax.dot_general(kvb[s, span, size:], g, NT, preferred_element_type=F32)
        ds = (w * (dp - delta)).astype(BF16)
        dk = jnp.dot(ds, q, preferred_element_type=F32)
        if first:
            dv_acc[s, span, :] = dv
            dk_acc[s, span, :] = dk
        else:
            dv_acc[s, span, :] += dv
            dk_acc[s, span, :] += dk
        if last:
            if s:
                send_combined(s)
            send_exchange(s, jnp.where(even[s], 2, 0))
            send_direct(s, jnp.where(even[s], 0, 2))
        part = jnp.dot(ktb[s, :, span], ds, preferred_element_type=F32)
        dqt = part if dqt is None else dqt + part
        if not finish:
            return dqt
        dq = (jnp.transpose(dqt) * scale).astype(BF16)
        for i, n in enumerate(heads):
            dqo[s, pl.ds(mult(p * rows, rows), rows), n * size:(n + 1) * size] = dq[i * rows:(i + 1) * rows]

    local[2].wait()
    local[3].wait()
    def arrival(s, k, t):
        copies = []
        for a, buf in enumerate((qb, gb)):
            part = buf.at[s, t, :, pl.ds(k * chunk_heads * size, chunk_heads * size)]
            copies.append(pltpu.make_async_copy(part, part, y_recv.at[s, k, t, a]))
        return copies

    started = {}
    for s in range(2):
        ktb[s, :, own_span] = jnp.transpose(kvb[s, own_span, :size])
        for k in range(chunks):
            started[s, k, -1] = compute(s, h, k, k == 0, False, [LOOK], None, False)
        forward(s)
    for i, t in enumerate(others):
        pltpu.make_async_copy(aux_r.at[t], aux_r.at[t], aux_recv_sem.at[t]).wait()
        if chunks > 1:
            started[0, 0, i] = compute(0, t, 0, False, False, [LOOK], None, False, arrival(0, 0, t))
    for s in range(2):
        wait_tile(s, 0)
        wait_tile(s, 2)
        ktb[s, :, :LOOK * block] = jnp.transpose(kvb[s, :LOOK * block, :size])
        for k in range(chunks):
            compute(s, h, k, k == 0, False, range(LOOK), started[s, k, -1])
        if s:
            send_combined(0)
        for k in range(chunks):
            for i, t in enumerate(others):
                last = k == chunks - 1 and i == n_kvh - 2
                if (s, k, i) in started:
                    compute(s, t, k, False, last, range(LOOK), started[s, k, i])
                else:
                    compute(s, t, k, False, last, range(LOOK + 1), arrival=arrival(s, k, t))
    early_sends = len(sent) - 3
    for cp in kvy + ysent + auxsent:
        cp.wait_send()
    for valid, cp in sent[:early_sends]:
        pl.when(valid)(cp.wait_send)
    for s in range(2):
        own = slice(LOOK * block, (LOOK + 1) * block)
        b = ids[s]
        dk_acc[s, own, :] = dk_acc[s, own, :] * scale
        lone = even[s] & (b + 3 >= n_ctx) & (b + 3 < n_blocks)
        for slot, valid in ((1, even[s] | (b + 3 < n_blocks)), (0, b + 2 < n_blocks), (3, lone)):
            @pl.when(valid)
            def _():
                pltpu.make_async_copy(rb.at[s, slot], rb.at[s, slot], d_recv.at[s, slot]).wait()
                dk_acc[s, own, :] += rb[s, slot, :, :size].astype(F32)
                dv_acc[s, own, :] += rb[s, slot, :, size:].astype(F32)

        dk_ref[s] = dk_acc[s, own, :].astype(BF16)
        dv_ref[s] = dv_acc[s, own, :].astype(BF16)

    for valid, cp in sent[early_sends:]:
        pl.when(valid)(cp.wait_send)


def write_out(*refs):
    copies = [
        pltpu.make_async_copy(refs[i], refs[3 + i], refs[6].at[i]) for i in range(3)
    ]
    for cp in copies:
        cp.start()
    for cp in copies:
        cp.wait()


def body(
    doc_lengths,
    queries,
    key_matrix,
    value_matrix,
    forward_output,
    output_cotangent,
    log_normalizer_rows,
):
    n_ctx, n_kvh = lax.axis_size("ctx"), lax.axis_size("kvh")
    rows = queries.shape[1]
    group = queries.shape[2] // key_matrix.shape[2]
    size = key_matrix.shape[2] // n_kvh
    block = rows * n_kvh
    width = group * size
    chunk_heads = max(1, min(group, 256 // rows))
    chunks = group // chunk_heads
    dims = (n_ctx, n_kvh, rows, group, size, chunk_heads, doc_lengths.shape[0])
    peers = n_kvh - 1
    lanes = chunk_heads * rows
    aux_rows = -(-4 * chunks // 8) * 8
    dma = pltpu.SemaphoreType.DMA
    anywhere = pl.BlockSpec(memory_space=pl.ANY)
    vmem = pl.BlockSpec(memory_space=pltpu.VMEM)
    grads = pl.pallas_call(
        functools.partial(kernel, dims),
        out_shape=(
            pltpu.VMEM((2, block, width), BF16),
            pltpu.VMEM((2, block, size), BF16),
            pltpu.VMEM((2, block, size), BF16),
        ),
        in_specs=[anywhere] * 7,
        out_specs=(vmem, vmem, vmem),
        scratch_shapes=[
            pltpu.SMEM(doc_lengths.shape, jnp.int32),
            pltpu.VMEM((2, group * n_kvh, rows), F32),
            pltpu.VMEM((2, n_kvh, rows, width), BF16),
            pltpu.VMEM((2, n_kvh, rows, width), BF16),
            pltpu.VMEM((2, rows, width * n_kvh), BF16),
            pltpu.VMEM((2, rows, width * n_kvh), BF16),
            pltpu.VMEM((2, (LOOK + 1) * block, 2 * size), BF16),
            pltpu.VMEM((2, size, (LOOK + 1) * block), BF16),
            pltpu.VMEM((2, (LOOK + 1) * block, size), F32),
            pltpu.VMEM((2, (LOOK + 1) * block, size), F32),
            pltpu.VMEM((2, 3, block, 2 * size), BF16),
            pltpu.VMEM((2, 4, block, 2 * size), BF16),
            pltpu.VMEM((n_kvh, aux_rows, lanes), F32),
            pltpu.VMEM((n_kvh, aux_rows, lanes), F32),
            dma((6,)),
            dma((2, 2)),
            dma((2, chunks, peers, 2)),
            dma((2, chunks, n_kvh, 2)),
            dma((2, peers, 2)),
            dma((2, n_kvh)),
            dma((2, 3)),
            dma((2, LOOK)),
            dma((peers,)),
            dma((n_kvh,)),
            dma((2, 3)),
            dma((2, 4)),
            pltpu.SemaphoreType.REGULAR((2,)),
        ],
        compiler_params=pltpu.CompilerParams(collective_id=0, has_side_effects=True),
    )(
        doc_lengths, jnp.transpose(log_normalizer_rows, (0, 2, 1)), queries, key_matrix, value_matrix,
        forward_output, output_cotangent,
    )
    return pl.pallas_call(
        write_out,
        out_shape=tuple(jax.ShapeDtypeStruct(x.shape, x.dtype) for x in grads),
        in_specs=[vmem] * 3,
        out_specs=[anywhere] * 3,
        scratch_shapes=[dma((3,))],
    )(*[pltpu.with_memory_space_constraint(x, pltpu.VMEM) for x in grads])


def solution(mesh):
    rows = P(None, ("ctx", "kvh"), None)
    return jax.shard_map(
        body,
        mesh=mesh,
        in_specs=(P(),) + (rows,) * 6,
        out_specs=(P(None, "ctx", "kvh"),) * 3,
        check_vma=False,
    )
```

```python
import functools

import jax
import jax.numpy as jnp
from jax import lax
from jax.experimental import pallas as pl
from jax.experimental.pallas import tpu as pltpu
from jax.sharding import PartitionSpec as P

LOOK = 3
MESH = pl.DeviceIdType.MESH
F32 = jnp.float32
BF16 = jnp.bfloat16
NT = (((1,), (1,)), ((), ()))


def row_sums(values, terms):
    ones = jnp.ones((8, values.shape[1]), BF16)
    total, rest = None, values
    for _ in range(terms):
        part = rest.astype(BF16)
        rest = rest - part.astype(F32)
        term = lax.dot_general(ones, part, NT, preferred_element_type=F32)
        total = term if total is None else total + term
    return total


def kernel(
    dims,
    docs_hbm, lse_hbm, q_hbm, k_hbm, v_hbm, o_hbm, g_hbm,
    dqo, dk_ref, dv_ref,
    docs_ref, lse_ref, qb, gb, gl, ol, kvb, ktb, dk_acc, dv_acc, sb, rb, aux_s, aux_r,
    loc_sem, kvl_sem, y_send, y_recv, kvy_send, kvy_recv, kv_send, kv_recv,
    aux_send_sem, aux_recv_sem, d_send, d_recv, gate,
):
    n_ctx, n_kvh, rows, group, size, chunk_heads, n_docs = dims
    block = n_kvh * rows
    width = group * size
    chunks = group // chunk_heads
    lanes = chunk_heads * rows
    n_blocks = 2 * n_ctx
    scale = size ** -0.5
    c = lax.axis_index("ctx")
    h = lax.axis_index("kvh")
    ids = (c, n_blocks - 1 - c)
    odd = lax.rem(c, 2)
    pair = c + 1 - 2 * odd
    even = (odd == 0, odd == 1)
    others = [lax.rem(h + i, n_kvh) for i in range(1, n_kvh)]

    def place(b):
        return jnp.where(b < n_ctx, b, n_blocks - 1 - b), jnp.where(b < n_ctx, 0, 1)

    def mult(x, m):
        return pl.multiple_of(x, m)

    def tile(j, p=None):
        if p is None:
            return pl.ds(mult(j * block, block), block)
        return pl.ds(mult(j * block + p * rows, rows), rows)

    barrier = pltpu.get_barrier_semaphore()
    leader = n_kvh - 1

    def signal(sem, **device):
        pl.semaphore_signal(sem, inc=1, device_id=device, device_id_type=MESH)

    @pl.when(h != leader)
    def _():
        signal(barrier, kvh=leader)

    @pl.when(h == leader)
    def _():
        if leader:
            pl.semaphore_wait(barrier, leader)
        for t in range(leader):
            signal(gate.at[0], kvh=t)

    own_cols = pl.ds(mult(h * width, width), width)
    own_key = pl.ds(mult(h * size, size), size)
    kv_local = []
    for s in range(2):
        for a, src in enumerate((k_hbm, v_hbm)):
            cp = pltpu.make_async_copy(
                src.at[s, :, own_key],
                kvb.at[s, tile(LOOK, h), pl.ds(a * size, size)],
                kvl_sem.at[s, a],
            )
            kv_local.append(cp)
    local = [
        pltpu.make_async_copy(g_hbm, gl, loc_sem.at[0]),
        pltpu.make_async_copy(o_hbm, ol, loc_sem.at[1]),
        pltpu.make_async_copy(q_hbm.at[:, :, own_cols], qb.at[:, h], loc_sem.at[2]),
        pltpu.make_async_copy(g_hbm.at[:, :, own_cols], gb.at[:, h], loc_sem.at[3]),
        pltpu.make_async_copy(lse_hbm, lse_ref, loc_sem.at[4]),
        pltpu.make_async_copy(docs_hbm, docs_ref, loc_sem.at[5]),
    ]

    def start_local():
        for cp in local[:2] + local[4:] + kv_local + local[2:4]:
            cp.start()

    @pl.when(h != leader)
    def _():
        start_local()
        pl.semaphore_wait(gate.at[0], 1)

    kvy, ysent, auxsent, sent = [], [], [], []
    for s in range(2):
        for i, t in enumerate(others):
            for a, src in enumerate((k_hbm, v_hbm)):
                cp = pltpu.make_async_remote_copy(
                    src.at[s, :, pl.ds(mult(t * size, size), size)],
                    kvb.at[s, tile(LOOK, h), pl.ds(a * size, size)],
                    kvy_send.at[s, i, a],
                    kvy_recv.at[s, h],
                    device_id={"kvh": t},
                    device_id_type=MESH,
                )
                cp.start()
                kvy.append(cp)

    def send_chunk(s, k):
        for i, t in enumerate(others):
            for a, (src, dst) in enumerate(((q_hbm, qb), (g_hbm, gb))):
                span = chunk_heads * size
                cp = pltpu.make_async_remote_copy(
                    src.at[s, :, pl.ds(mult(t * width + k * span, span), span)],
                    dst.at[s, h, :, pl.ds(k * span, span)],
                    y_send.at[s, k, i, a],
                    y_recv.at[s, k, h, a],
                    device_id={"kvh": t},
                    device_id_type=MESH,
                )
                cp.start()
                ysent.append(cp)

    pl.when(h == leader)(start_local)
    send_chunk(0, 0)
    near = [(ctx, (ctx >= 0) & (ctx < n_ctx)) for ctx in (c - 2, c + 2, c - 3 + 6 * odd)]

    @pl.when(h == 0)
    def _():
        signal(barrier, ctx=pair)
        for ctx, inside in near:
            @pl.when(inside)
            def _():
                signal(barrier, ctx=ctx)

    for s in range(2):
        for d in range(1, LOOK + 1):
            @pl.when(ids[s] - d < 0)
            def _():
                kvb[s, (LOOK - d) * block:(LOOK - d + 1) * block, :] = jnp.zeros(
                    (block, 2 * size), BF16
                )
    def send(valid, src, dst, send_sem, recv_sem, ctx):
        cp = pltpu.make_async_remote_copy(
            src, dst, send_sem, recv_sem, device_id={"ctx": ctx}, device_id_type=MESH
        )
        pl.when(valid)(cp.start)
        sent.append((valid, cp))

    def spread(s):
        b, src = ids[s], kvb.at[s, tile(LOOK), :]
        ctx, half = place(b + 2)
        send(
            b + 2 < n_blocks, src, kvb.at[half, tile(1), :],
            kv_send.at[s, 0], kv_recv.at[half, 1], ctx,
        )
        ctx, half = place(b + 3)
        j = jnp.where(even[s], 2, 0)
        ctx, half = jnp.where(even[s], pair, ctx), jnp.where(even[s], s, half)
        send(
            even[s] | (b + 3 < n_blocks), src, kvb.at[half, tile(j), :],
            kv_send.at[s, 1], kv_recv.at[half, j], ctx,
        )

    def wait_tile(s, j):
        part = kvb.at[s, tile(j), :]
        pl.when(ids[s] - (LOOK - j) >= 0)(
            pltpu.make_async_copy(part, part, kv_recv.at[s, j]).wait
        )

    def forward(s):
        wait_tile(s, 1)
        j = jnp.where(even[s], 0, 2)
        send(
            ids[s] >= 2, kvb.at[s, tile(1), :], kvb.at[s, tile(j), :],
            kv_send.at[s, 2], kv_recv.at[s, j], pair,
        )

    local[0].wait()
    local[1].wait()
    local[4].wait()

    def fill_aux(g):
        cols = pl.ds(mult(g * width, width), width)
        for s in range(2):
            prods = gl[s, :, cols].astype(F32) * ol[s, :, cols].astype(F32)
            delta = row_sums(
                jnp.concatenate([prods[:, i * size:(i + 1) * size] for i in range(group)], axis=0), 2
            )
            for k in range(chunks):
                r = 2 * (s * chunks + k)
                aux_s[g, r + 1:r + 2, :] = delta[:1, k * lanes:(k + 1) * lanes]
                lse = lse_ref[s, pl.ds(mult(g * group + k * chunk_heads, chunk_heads), chunk_heads), :]
                for i in range(chunk_heads):
                    aux_s[g, r:r + 1, i * rows:(i + 1) * rows] = lse[i:i + 1]

    for i, t in enumerate(others):
        fill_aux(t)
        cp = pltpu.make_async_remote_copy(
            aux_s.at[t], aux_r.at[h], aux_send_sem.at[i], aux_recv_sem.at[h],
            device_id={"kvh": t}, device_id_type=MESH,
        )
        cp.start()
        auxsent.append(cp)
    for s in range(2):
        for k in range(chunks):
            if s + k:
                send_chunk(s, k)
    @pl.when(h == 0)
    def _():
        count = jnp.int32(1)
        for _, inside in near:
            count = count + inside.astype(jnp.int32)
        pl.semaphore_wait(barrier, count)
        for t in range(1, n_kvh):
            signal(gate.at[1], kvh=t)

    @pl.when(h != 0)
    def _():
        pl.semaphore_wait(gate.at[1], 1)

    for cp in kv_local:
        cp.wait()
    for s in range(2):
        for t in others:
            part = kvb.at[s, tile(LOOK, t), :]
            pltpu.make_async_copy(part, part, kvy_recv.at[s, t]).wait()
        spread(s)
    fill_aux(h)
    aux_r[h] = aux_s[h]

    own_span = slice(LOOK * block, (LOOK + 1) * block)
    local[5].wait()
    ends, total = [], jnp.int32(0)
    for i in range(n_docs):
        total = total + docs_ref[i]
        ends.append(total)
    spot = lax.broadcasted_iota(jnp.int32, (1, lanes), 1) % rows
    key_spot = lax.broadcasted_iota(jnp.int32, (block, lanes), 0)

    def stage(s, slot, dk, dv):
        sb[s, slot, :, :size] = (dk * scale).astype(BF16)
        sb[s, slot, :, size:] = dv.astype(BF16)

    def send_exchange(s, j):
        stage(s, 0, dk_acc[s, tile(j), :], dv_acc[s, tile(j), :])
        send(ids[s] >= 2, sb.at[s, 0], rb.at[s, 2], d_send.at[s, 0], d_recv.at[s, 2], pair)

    def send_direct(s, j):
        stage(s, 1, dk_acc[s, tile(j), :], dv_acc[s, tile(j), :])
        b = ids[s]
        ctx, half = place(b - 3)
        ctx, half = jnp.where(even[s], ctx, pair), jnp.where(even[s], half, s)
        send(
            (~even[s]) | (b - 3 >= 0), sb.at[s, 1], rb.at[half, 1],
            d_send.at[s, 1], d_recv.at[half, 1], ctx,
        )

    def send_combined(s):
        b = ids[s]
        ctx, half = place(b - 2)

        @pl.when(b >= 2)
        def _():
            pltpu.make_async_copy(rb.at[s, 2], rb.at[s, 2], d_recv.at[s, 2]).wait()
            sb[s, 2, :, :size] = (
                dk_acc[s, block:2 * block, :] * scale + rb[s, 2, :, :size].astype(F32)
            ).astype(BF16)
            sb[s, 2, :, size:] = (
                dv_acc[s, block:2 * block, :] + rb[s, 2, :, size:].astype(F32)
            ).astype(BF16)

        send(b >= 2, sb.at[s, 2], rb.at[half, 0], d_send.at[s, 2], d_recv.at[half, 0], ctx)

    def compute(s, p, k, first, last, tiles, dqt=None, finish=True, arrival=None):
        heads = range(k * chunk_heads, (k + 1) * chunk_heads)
        if arrival:
            arrival[0].wait()
        q = jnp.concatenate([qb[s, p, :, n * size:(n + 1) * size] for n in heads], axis=0)
        r = 2 * (s * chunks + k)
        norm = aux_r[p, r:r + 1, :]
        delta = aux_r[p, r + 1:r + 2, :]
        pos = ids[s] * block + p * rows + spot
        start = jnp.zeros_like(pos)
        for end in ends:
            start = jnp.where(pos >= end, end, start)
        base = (ids[s] - LOOK) * block
        pos, start = pos - base, start - base
        if last:
            tiles = [jnp.where(even[s], 2, 0), jnp.where(even[s], 0, 2), 1, LOOK]
        lo, hi = (tiles[0], tiles[-1]) if not last else (0, LOOK)
        span = slice(lo * block, (hi + 1) * block)
        size_k = (hi + 1 - lo) * block
        st = lax.dot_general(kvb[s, span, :size], q, NT, preferred_element_type=F32)
        t = lax.broadcasted_iota(jnp.int32, (size_k, lanes), 0) + lo * block
        allowed = t >= start
        if hi == LOOK:
            allowed = allowed & (t <= pos)
        w = jnp.where(allowed, jnp.exp(st * scale - norm), 0.0)
        if arrival:
            arrival[1].wait()
        g = jnp.concatenate([gb[s, p, :, n * size:(n + 1) * size] for n in heads], axis=0)
        dv = jnp.dot(w.astype(BF16), g, preferred_element_type=F32)
        dp = lax.dot_general(kvb[s, span, size:], g, NT, preferred_element_type=F32)
        ds = (w * (dp - delta)).astype(BF16)
        dk = jnp.dot(ds, q, preferred_element_type=F32)
        if first:
            dv_acc[s, span, :] = dv
            dk_acc[s, span, :] = dk
        else:
            dv_acc[s, span, :] += dv
            dk_acc[s, span, :] += dk
        part = jnp.dot(ktb[s, :, span], ds, preferred_element_type=F32)
        dqt = part if dqt is None else dqt + part
        if last:
            send_exchange(s, jnp.where(even[s], 2, 0))
            send_direct(s, jnp.where(even[s], 0, 2))
        if last and s:
            send_combined(s)
        if not finish:
            return dqt
        dq = (jnp.transpose(dqt) * scale).astype(BF16)
        for i, n in enumerate(heads):
            dqo[s, pl.ds(mult(p * rows, rows), rows), n * size:(n + 1) * size] = dq[i * rows:(i + 1) * rows]

    local[2].wait()
    local[3].wait()
    def arrival(s, k, t):
        copies = []
        for a, buf in enumerate((qb, gb)):
            part = buf.at[s, t, :, pl.ds(k * chunk_heads * size, chunk_heads * size)]
            copies.append(pltpu.make_async_copy(part, part, y_recv.at[s, k, t, a]))
        return copies

    started = {}
    for s in range(2):
        ktb[s, :, own_span] = jnp.transpose(kvb[s, own_span, :size])
        for k in range(chunks):
            started[s, k, -1] = compute(s, h, k, k == 0, False, [LOOK], None, False)
        forward(s)
    for i, t in enumerate(others):
        pltpu.make_async_copy(aux_r.at[t], aux_r.at[t], aux_recv_sem.at[t]).wait()
        if chunks > 1:
            started[0, 0, i] = compute(0, t, 0, False, False, [LOOK], None, False, arrival(0, 0, t))
    for s in range(2):
        wait_tile(s, 0)
        wait_tile(s, 2)
        ktb[s, :, :LOOK * block] = jnp.transpose(kvb[s, :LOOK * block, :size])
        for k in range(chunks):
            compute(s, h, k, k == 0, False, range(LOOK), started[s, k, -1])
        if s:
            send_combined(0)
        for k in range(chunks):
            for i, t in enumerate(others):
                last = k == chunks - 1 and i == n_kvh - 2
                if (s, k, i) in started:
                    compute(s, t, k, False, last, range(LOOK), started[s, k, i])
                else:
                    compute(s, t, k, False, last, range(LOOK + 1), arrival=arrival(s, k, t))
    early_sends = len(sent) - 3
    for cp in kvy + ysent + auxsent:
        cp.wait_send()
    for valid, cp in sent[:early_sends]:
        pl.when(valid)(cp.wait_send)
    for s in range(2):
        own = slice(LOOK * block, (LOOK + 1) * block)
        b = ids[s]
        dk_acc[s, own, :] = dk_acc[s, own, :] * scale
        for slot, valid in ((1, even[s] | (b + 3 < n_blocks)), (0, b + 2 < n_blocks)):
            @pl.when(valid)
            def _():
                pltpu.make_async_copy(rb.at[s, slot], rb.at[s, slot], d_recv.at[s, slot]).wait()
                dk_acc[s, own, :] += rb[s, slot, :, :size].astype(F32)
                dv_acc[s, own, :] += rb[s, slot, :, size:].astype(F32)

        dk_ref[s] = dk_acc[s, own, :].astype(BF16)
        dv_ref[s] = dv_acc[s, own, :].astype(BF16)

    for valid, cp in sent[early_sends:]:
        pl.when(valid)(cp.wait_send)


def write_out(*refs):
    copies = [
        pltpu.make_async_copy(refs[i], refs[3 + i], refs[6].at[i]) for i in range(3)
    ]
    for cp in copies:
        cp.start()
    for cp in copies:
        cp.wait()


def body(
    doc_lengths,
    queries,
    key_matrix,
    value_matrix,
    forward_output,
    output_cotangent,
    log_normalizer_rows,
):
    n_ctx, n_kvh = lax.axis_size("ctx"), lax.axis_size("kvh")
    rows = queries.shape[1]
    group = queries.shape[2] // key_matrix.shape[2]
    size = key_matrix.shape[2] // n_kvh
    block = rows * n_kvh
    width = group * size
    chunk_heads = max(1, min(group, 256 // rows))
    chunks = group // chunk_heads
    dims = (n_ctx, n_kvh, rows, group, size, chunk_heads, doc_lengths.shape[0])
    peers = n_kvh - 1
    lanes = chunk_heads * rows
    aux_rows = -(-4 * chunks // 8) * 8
    dma = pltpu.SemaphoreType.DMA
    anywhere = pl.BlockSpec(memory_space=pl.ANY)
    vmem = pl.BlockSpec(memory_space=pltpu.VMEM)
    grads = pl.pallas_call(
        functools.partial(kernel, dims),
        out_shape=(
            pltpu.VMEM((2, block, width), BF16),
            pltpu.VMEM((2, block, size), BF16),
            pltpu.VMEM((2, block, size), BF16),
        ),
        in_specs=[anywhere] * 7,
        out_specs=(vmem, vmem, vmem),
        scratch_shapes=[
            pltpu.SMEM(doc_lengths.shape, jnp.int32),
            pltpu.VMEM((2, group * n_kvh, rows), F32),
            pltpu.VMEM((2, n_kvh, rows, width), BF16),
            pltpu.VMEM((2, n_kvh, rows, width), BF16),
            pltpu.VMEM((2, rows, width * n_kvh), BF16),
            pltpu.VMEM((2, rows, width * n_kvh), BF16),
            pltpu.VMEM((2, (LOOK + 1) * block, 2 * size), BF16),
            pltpu.VMEM((2, size, (LOOK + 1) * block), BF16),
            pltpu.VMEM((2, (LOOK + 1) * block, size), F32),
            pltpu.VMEM((2, (LOOK + 1) * block, size), F32),
            pltpu.VMEM((2, 3, block, 2 * size), BF16),
            pltpu.VMEM((2, 3, block, 2 * size), BF16),
            pltpu.VMEM((n_kvh, aux_rows, lanes), F32),
            pltpu.VMEM((n_kvh, aux_rows, lanes), F32),
            dma((6,)),
            dma((2, 2)),
            dma((2, chunks, peers, 2)),
            dma((2, chunks, n_kvh, 2)),
            dma((2, peers, 2)),
            dma((2, n_kvh)),
            dma((2, 3)),
            dma((2, LOOK)),
            dma((peers,)),
            dma((n_kvh,)),
            dma((2, 3)),
            dma((2, 3)),
            pltpu.SemaphoreType.REGULAR((2,)),
        ],
        compiler_params=pltpu.CompilerParams(collective_id=0, has_side_effects=True),
    )(
        doc_lengths, jnp.transpose(log_normalizer_rows, (0, 2, 1)), queries, key_matrix, value_matrix,
        forward_output, output_cotangent,
    )
    return pl.pallas_call(
        write_out,
        out_shape=tuple(jax.ShapeDtypeStruct(x.shape, x.dtype) for x in grads),
        in_specs=[vmem] * 3,
        out_specs=[anywhere] * 3,
        scratch_shapes=[dma((3,))],
    )(*[pltpu.with_memory_space_constraint(x, pltpu.VMEM) for x in grads])


def solution(mesh):
    rows = P(None, ("ctx", "kvh"), None)
    return jax.shard_map(
        body,
        mesh=mesh,
        in_specs=(P(),) + (rows,) * 6,
        out_specs=(P(None, "ctx", "kvh"),) * 3,
        check_vma=False,
    )
```
